128 devices in a mesh: row: 8 (over y_hi, x), col: 16 (over z, y_lo, core).
Axes of the slice: x: 4, y: 4 (y_hi: 2, y_lo: 2; y = y_hi * 2 + y_lo), z: 4, core: 2. Of those that a mesh axis runs over, the one named last changes fastest.
Arguments:
- normals: float32 [2048, 16384], P('row', 'col'), may hold values from -6 to 6
- factor: float32 [16384, 16384], P('row', 'col'), as said below
- cell_entity: int32 [16384], P('row'), may hold values from 0 to 1023
- scale: float32 [16384], P('row'), may hold values from 0.25 to 2
- volatility: float32 [16384], P('row'), may hold values from 0.1 to 0.6
- retention: int32 [16384], P('row'), may hold values from 1 to 11
- limit: int32 [16384], P('row'), may hold values from 1 to 15
Outputs:
- entity_loss: float32 [2, 2048, 1024], P(None, 'col', 'row')
The draws below stay inside these ranges and needn't reach their ends.
Inputs may be any that keep to these rules, and one draw needn't show every extreme that they name: factor is zero above the diagonal and one on it.
All inputs are finite; a program needn't handle non-finite values.
Results may differ from the reference program's by a relative error of at most 0.000078.
Values sent between devices are 32-bit elements; how exact they have to be, the bound alone decides.
No kernel may reach another device: no remote copies, remote signals or barrier semaphores. Data moves between devices by JAX's collectives and lax.ppermute only.
A program may use at most 128 MiB of HBM per device.

```python
import math
import jax
import jax.numpy as jnp
from jax import lax

CELLS = 16384
ENT = 1024
SCEN = 2048


def draw_factor(key, part):
    rows = jnp.arange(CELLS, dtype=jnp.int32)[:, None]
    cols = jnp.arange(CELLS, dtype=jnp.int32)[None, :]
    values = jax.random.normal(key, (CELLS, CELLS), jnp.float32) * (2.0 / CELLS ** 0.5)
    lower = jnp.where(cols < rows, values, 0.0)
    return jnp.where(cols == rows, 1.0, lower).astype(jnp.float32)


def plant(drawn, rng, low, high):
    longest = drawn.shape.index(max(drawn.shape))
    spots = []
    for shift in (0, 1):
        where = [jax.random.randint(jax.random.fold_in(rng, axis), (), 0, length) for axis, length in enumerate(drawn.shape)]
        where[longest] = (where[longest] + shift) % drawn.shape[longest]
        spots.append(tuple(where))
    return drawn.at[spots[0]].set(low).at[spots[1]].set(high)


def block_levels(rng, dims, pieces, smallest, largest):
    level, own = 1.0, jax.random.fold_in(rng, 6)
    for dim, blocks in pieces:
        draws = jnp.exp(jax.random.uniform(jax.random.fold_in(own, dim), (blocks,), jnp.float32, smallest / len(pieces), largest / len(pieces)))
        level = level * jnp.repeat(draws, dims[dim] // blocks).reshape([-1 if axis == dim else 1 for axis in range(len(dims))])
    return level


def gaussian(rng, extent, deviation, most, cuts=(), kind=jnp.bfloat16):
    drawn = jax.random.normal(rng, extent, jnp.float32) * deviation
    if len(cuts) > 0:
        drawn = block_levels(rng, extent, cuts, -0.22, 0.18) * drawn
    return jnp.clip(drawn, min=-most, max=most).astype(kind)


def setup_inputs(seed: int = 0) -> dict:
    key_list = jax.random.split(jax.random.key(seed), 8)
    normals = gaussian(key_list[0], (SCEN, CELLS), 1.0, 6.0, ((0, 8), (1, 16)), jnp.float32)
    factor = draw_factor(jax.random.fold_in(key_list[7], 71), 0)
    cell_entity = plant(jax.random.randint(key_list[2], (CELLS,), 0, ENT), jax.random.fold_in(key_list[2], 1), 0, ENT - 1).astype(jnp.int32)
    scale = jnp.clip(jnp.exp(math.log(2.0) - 2.0794415 * jax.random.uniform(key_list[3], (CELLS,), jnp.float32) ** block_levels(key_list[3], (CELLS,), ((0, 8),), -0.2, 0.2)), 0.25, 2.0)
    volatility = jnp.clip(jnp.exp(math.log(0.6) - 1.7917595 * jax.random.uniform(key_list[4], (CELLS,), jnp.float32) ** block_levels(key_list[4], (CELLS,), ((0, 8),), -0.2, 0.2)), 0.1, 0.6)
    retention = plant(jax.random.randint(key_list[5], (CELLS,), 1, 12), jax.random.fold_in(key_list[5], 1), 1, 11).astype(jnp.int32)
    limit = plant(jax.random.randint(key_list[6], (CELLS,), 1, 16), jax.random.fold_in(key_list[6], 1), 1, 15).astype(jnp.int32)
    return {"normals": normals, "factor": factor, "cell_entity": cell_entity, "scale": scale, "volatility": volatility, "retention": retention, "limit": limit}


def reference(normals, factor, cell_entity, scale, volatility, retention, limit):
    norms = lax.optimization_barrier(jnp.sum(factor * factor, axis=1))
    mixed = lax.dot_general(normals, factor, (((1,), (1,)), ((), ())), precision=lax.Precision.HIGHEST, preferred_element_type=jnp.float32)
    correlated = mixed * lax.rsqrt(norms)[None, :]
    ground = scale[None, :] * jnp.exp(volatility[None, :] * correlated)
    floor_level = 0.25 * retention.astype(jnp.float32)
    cover = 0.25 * limit.astype(jnp.float32)
    ceded = jnp.minimum(jnp.maximum(ground - floor_level[None, :], 0.0), cover[None, :])
    net = ground - ceded
    onehot = (cell_entity[:, None] == jnp.arange(ENT, dtype=jnp.int32)[None, :]).astype(jnp.float32)
    stacked = jnp.stack([net, ceded])
    return jnp.einsum('ksc,ce->kse', stacked, onehot, precision=lax.Precision.HIGHEST)
```

```python
import functools

import jax
import jax.numpy as jnp
import numpy as np
from jax import lax
from jax.experimental import pallas as pl
from jax.experimental.pallas import tpu as pltpu
from jax.sharding import PartitionSpec as P

ENT = 1024
ROWS = (48, 48, 32)
OFFS = (0, 48, 96)
TILE = 256
COLS = (768, 768, 512)
COFF = (0, 768, 1536)
BOTH = ("row", "col")


def unflat(i):
    row, col = divmod(i, 16)
    return row // 4, row % 4, col // 4, col // 2 % 2, col % 2


def flat(yh, x, z, yl, core):
    return (yh * 4 + x) * 16 + z * 4 + yl * 2 + core


def perm(step):
    return [(i, flat(*step(*unflat(i)))) for i in range(128)]


CORE = perm(lambda yh, x, z, yl, c: (yh, x, z, yl, 1 - c))
ROW_DIMS = (
    perm(lambda yh, x, z, yl, c: (yh, x ^ 1, z, yl, c)),
    perm(lambda yh, x, z, yl, c: (yh, 3 - x, z, yl, c)),
    perm(lambda yh, x, z, yl, c: (1 - yh, x, z, yl, c)),
)
COL_DIMS = (
    perm(lambda yh, x, z, yl, c: (yh, x, z ^ 1, yl, c)),
    perm(lambda yh, x, z, yl, c: (yh, x, 3 - z, yl, c)),
    perm(lambda yh, x, z, yl, c: (yh, x, z, 1 - yl, c)),
)


def gray(v):
    return v ^ (v >> 1)


def ungray(v):
    return (v & 2) | ((v ^ (v >> 1)) & 1)


def tables():
    out = np.zeros((128, 3, 2, 4, 3), np.int32)
    for i in range(128):
        yh, x, z, yl, _ = unflat(i)
        here_r, here_c = gray(x) | yh << 2, gray(z) | yl << 2
        e_of_d = {}
        for e in range(8):
            h = here_r ^ e
            source = (h >> 2) * 4 + ungray(h & 3)
            e_of_d[(gray(source >> 1) | (source & 1) << 2) ^ here_c] = e
        for q in range(3):
            for m in range(8):
                bits = [1 - (m >> 2 & 1), 1 - (m >> 1 & 1), 1 - (m & 1)]
                e = e_of_d[sum(b << (q + s) % 3 for s, b in enumerate(bits))]
                for p in range(3):
                    out[i, q, m // 4, m % 4, p] = sum(
                        (e >> (p + s) % 3 & 1) << s for s in range(3)
                    )
    return out.reshape(128, 6, 12)


def permute(x, pairs):
    return lax.ppermute(x, BOTH, pairs)


def split(x):
    high = lax.reduce_precision(x, 8, 7)
    return high.astype(jnp.bfloat16), (x - high).astype(jnp.bfloat16)


def mm_kernel(tbl, *refs):
    blocks, (fho, flo, fhp, flp, out, high, low) = refs[:12], refs[12:]

    @pl.when(pl.program_id(0) == 0)
    def _():
        for i in range(4):
            for p in range(3):
                v = blocks[i * 3 + p][0]
                h = v.astype(jnp.bfloat16)
                at = pl.ds(i * 128 + OFFS[p], ROWS[p])
                high[at, :] = h
                low[at, :] = (v - h.astype(jnp.float32)).astype(jnp.bfloat16)

    dot = functools.partial(
        lax.dot_general,
        dimension_numbers=(((1,), (1,)), ((), ())),
        preferred_element_type=jnp.float32,
    )
    own, far = pl.ds(0, 1024), pl.ds(1024, 1024)
    acc = dot(high[:, own], fho[...]) + dot(high[:, far], fhp[...])
    acc += dot(high[:, own], flo[...]) + dot(high[:, far], flp[...])
    acc += dot(low[:, own], fho[...]) + dot(low[:, far], fhp[...])
    out[...] = acc.reshape(4, 128, TILE)


def mm(tbl, gathered, factors, q):
    tiles, first = COLS[q] // TILE, COFF[q] // TILE
    specs = [
        pl.BlockSpec((1, ROWS[p], 2048), lambda t, tb, k=i * 3 + p: (tb[k], 0, 0))
        for i in range(4)
        for p in range(3)
    ]
    specs += [pl.BlockSpec((TILE, 1024), lambda t, tb: (first + t, 0))] * 4
    return pl.pallas_call(
        mm_kernel,
        out_shape=jax.ShapeDtypeStruct((4, 128, COLS[q]), jnp.float32),
        grid_spec=pltpu.PrefetchScalarGridSpec(
            num_scalar_prefetch=1,
            grid=(tiles,),
            in_specs=specs,
            out_specs=pl.BlockSpec((4, 128, TILE), lambda t, tb: (0, 0, t)),
            scratch_shapes=[pltpu.VMEM((512, 2048), jnp.bfloat16)] * 2,
        ),
        cost_estimate=pl.CostEstimate(
            flops=2 * 3 * 512 * 2048 * COLS[q],
            bytes_accessed=4 * 2**20 + COLS[q] * (2048 * 4 + 2048),
            transcendentals=0,
        ),
        compiler_params=pltpu.CompilerParams(vmem_limit_bytes=40 * 2**20),
    )(tbl, *(gathered * 4), *factors)


def body(normals, factor, cell_entity, scale, volatility, retention, limit):
    row, col = lax.axis_index("row"), lax.axis_index("col")
    core = col % 2
    tbl = lax.dynamic_index_in_dim(jnp.asarray(tables()), row * 16 + col, 0, False)

    given = permute(lax.dynamic_slice_in_dim(normals, (1 - core) * 128, 128, 0), CORE)
    kept = lax.dynamic_slice_in_dim(normals, core * 128, 128, 0)
    block = jnp.concatenate([kept, given], axis=1)
    far_factor = permute(factor, CORE)

    gathered = [block[None, OFFS[p] : OFFS[p] + ROWS[p]] for p in range(3)]
    for s in range(3):
        for p in range(3):
            came = permute(gathered[p], ROW_DIMS[(p + s) % 3])
            gathered[p] = jnp.concatenate([gathered[p], came], axis=0)

    fho, flo = split(factor)
    fhp, flp = split(far_factor)
    factors = (fho, flo, fhp, flp)

    norms = jnp.sum(factor * factor, axis=1) + jnp.sum(far_factor * far_factor, axis=1)
    for d in range(3):
        norms = norms + permute(norms, COL_DIMS[d])

    sent = [mm(tbl[2 * q], gathered, factors, q) for q in range(3)]
    came = [permute(sent[q], COL_DIMS[q]) for q in range(3)]
    kept = [mm(tbl[2 * q + 1], gathered, factors, q) for q in range(3)]
    second = [permute(kept[q][:2] + came[q][:2], COL_DIMS[(q + 1) % 3]) for q in range(3)]
    held = [kept[q][2:] + came[q][2:] + second[q] for q in range(3)]
    third = [permute(held[q][0], COL_DIMS[(q + 2) % 3]) for q in range(3)]
    mixed = jnp.concatenate([held[q][1] + third[q] for q in range(3)], axis=1)

    correlated = mixed * lax.rsqrt(norms)[None, :]
    ground = scale[None, :] * jnp.exp(volatility[None, :] * correlated)
    floor_level = 0.25 * retention.astype(jnp.float32)
    cover = 0.25 * limit.astype(jnp.float32)
    ceded = jnp.minimum(jnp.maximum(ground - floor_level[None, :], 0.0), cover[None, :])
    net = ground - ceded
    onehot = (cell_entity[:, None] == jnp.arange(ENT, dtype=jnp.int32)[None, :]).astype(jnp.float32)
    sums = jnp.einsum("ksc,ce->kse", jnp.stack([net, ceded]), onehot, precision=lax.Precision.HIGH)
    parts = lax.all_to_all(sums, "row", split_axis=2, concat_axis=0, tiled=True)
    return jnp.sum(parts.reshape(8, 2, 128, 128), axis=0)


def solution(mesh):
    return jax.shard_map(
        body,
        mesh=mesh,
        in_specs=(
            P("row", "col"),
            P("row", "col"),
            P("row"),
            P("row"),
            P("row"),
            P("row"),
            P("row"),
        ),
        out_specs=P(None, "col", "row"),
        check_vma=False,
    )
```

```python
import functools

import jax
import jax.numpy as jnp
import numpy as np
from jax import lax
from jax.experimental import pallas as pl
from jax.experimental.pallas import tpu as pltpu
from jax.sharding import PartitionSpec as P


ENT = 1024
CHUNKS = 2
ROWS = 128 // CHUNKS
DEPTH = (768, 640, 640)
DOFF = (0, 768, 1408)
TILE = 256
COLS = (768, 768, 512)
COFF = (0, 768, 1536)
BOTH = ("row", "col")


def unflat(i):
    row, col = divmod(i, 16)
    return row // 4, row % 4, col // 4, col // 2 % 2, col % 2


def flat(yh, x, z, yl, core):
    return (yh * 4 + x) * 16 + z * 4 + yl * 2 + core


def perm(step):
    return [(i, flat(*step(*unflat(i)))) for i in range(128)]


CORE = perm(lambda yh, x, z, yl, c: (yh, x, z, yl, 1 - c))
ROW_DIMS = (
    perm(lambda yh, x, z, yl, c: (yh, x ^ 1, z, yl, c)),
    perm(lambda yh, x, z, yl, c: (yh, 3 - x, z, yl, c)),
    perm(lambda yh, x, z, yl, c: (1 - yh, x, z, yl, c)),
)
COL_DIMS = (
    perm(lambda yh, x, z, yl, c: (yh, x, z ^ 1, yl, c)),
    perm(lambda yh, x, z, yl, c: (yh, x, 3 - z, yl, c)),
    perm(lambda yh, x, z, yl, c: (yh, x, z, 1 - yl, c)),
)


def gray(v):
    return v ^ (v >> 1)


def ungray(v):
    return (v & 2) | ((v ^ (v >> 1)) & 1)


def tables():
    out = np.zeros((128, 3, 2, 4, 3), np.int32)
    for i in range(128):
        yh, x, z, yl, _ = unflat(i)
        here_r, here_c = gray(x) | yh << 2, gray(z) | yl << 2
        e_of_d = {}
        for e in range(8):
            h = here_r ^ e
            source = (h >> 2) * 4 + ungray(h & 3)
            e_of_d[(gray(source >> 1) | (source & 1) << 2) ^ here_c] = e
        for q in range(3):
            for m in range(8):
                bits = [1 - (m >> 2 & 1), 1 - (m >> 1 & 1), 1 - (m & 1)]
                e = e_of_d[sum(b << (q + s) % 3 for s, b in enumerate(bits))]
                for p in range(3):
                    out[i, q, m // 4, m % 4, p] = sum(
                        (e >> (p + s) % 3 & 1) << s for s in range(3)
                    )
    return out.reshape(128, 72)


def permute(x, pairs):
    return lax.ppermute(x, BOTH, pairs)


def split(x):
    high = lax.reduce_precision(x, 8, 7)
    return high.astype(jnp.bfloat16), (x - high).astype(jnp.bfloat16)


def mm_kernel(qs, tbl, *refs):
    blocks, factors = refs[:12], refs[12:16]
    outs, both = refs[16 : 16 + len(qs)], refs[16 + len(qs)]
    fho, flo, fhp, flp = factors
    m = 4 * ROWS
    t = pl.program_id(0)
    first = 0
    starts = []
    for q in qs:
        starts.append(first)
        first += COLS[q] // TILE

    @pl.when(functools.reduce(jnp.logical_or, [t == v for v in starts]))
    def _():
        for i in range(4):
            for p in range(3):
                v = blocks[i * 3 + p][0]
                h = v.astype(jnp.bfloat16)
                cols = pl.ds(DOFF[p], DEPTH[p])
                both[pl.ds(i * ROWS, ROWS), cols] = h
                both[pl.ds(m + i * ROWS, ROWS), cols] = (v - h.astype(jnp.float32)).astype(jnp.bfloat16)

    dot = functools.partial(
        lax.dot_general,
        dimension_numbers=(((1,), (1,)), ((), ())),
        preferred_element_type=jnp.float32,
    )
    own, far, high = pl.ds(0, 1024), pl.ds(1024, 1024), pl.ds(0, m)
    acc = dot(both[:, own], fho[...]) + dot(both[:, far], fhp[...])
    low = dot(both[high, own], flo[...]) + dot(both[high, far], flp[...])
    acc = (acc[:m] + (acc[m:] + low)).reshape(4, ROWS, TILE)
    for k, q in enumerate(qs):
        if len(qs) == 1:
            outs[k][...] = acc
        else:

            @pl.when((t >= starts[k]) & (t < starts[k] + COLS[q] // TILE))
            def _(k=k):
                outs[k][...] = acc


def mm(tbl, gathered, factors, qs):
    sizes = [COLS[q] // TILE for q in qs]
    starts = [sum(sizes[:k]) for k in range(len(qs))]

    def which(t):
        return sum(((t >= v).astype(jnp.int32) for v in starts[1:]), jnp.int32(0))

    specs = [
        pl.BlockSpec((1, ROWS, DEPTH[p]), lambda t, tb, k=i * 3 + p: (tb[which(t) * 12 + k], 0, 0))
        for i in range(4)
        for p in range(3)
    ]
    specs += [pl.BlockSpec((TILE, 1024), lambda t, tb: (COFF[qs[0]] // TILE + t, 0))] * 4
    return pl.pallas_call(
        functools.partial(mm_kernel, qs),
        out_shape=[jax.ShapeDtypeStruct((4, ROWS, COLS[q]), jnp.float32) for q in qs],
        grid_spec=pltpu.PrefetchScalarGridSpec(
            num_scalar_prefetch=1,
            grid=(sum(sizes),),
            in_specs=specs,
            out_specs=[
                pl.BlockSpec(
                    (4, ROWS, TILE),
                    lambda t, tb, k=k: (0, 0, jnp.clip(t - starts[k], 0, sizes[k] - 1)),
                )
                for k in range(len(qs))
            ],
            scratch_shapes=[pltpu.VMEM((8 * ROWS, 2048), jnp.bfloat16)],
        ),
        cost_estimate=pl.CostEstimate(
            flops=2 * 3 * 4 * ROWS * 2048 * sum(sizes) * TILE,
            bytes_accessed=4 * ROWS * 2048 * 4 + sum(sizes) * TILE * (2048 * 4 + 16 * ROWS),
            transcendentals=0,
        ),
        compiler_params=pltpu.CompilerParams(vmem_limit_bytes=32 * 2**20),
    )(tbl, *(gathered * 4), *factors)


def step(normals, factor, cell_entity, scale, volatility, retention, limit):
    row, col = lax.axis_index("row"), lax.axis_index("col")
    core = col & 1
    tbl = lax.dynamic_index_in_dim(jnp.asarray(tables()), row * 16 + col, 0, False).reshape(6, 12)

    given = permute(lax.dynamic_slice_in_dim(normals, (1 - core) * 128, 128, 0), CORE)
    kept = lax.dynamic_slice_in_dim(normals, core * 128, 128, 0)
    factor, given = lax.optimization_barrier((factor, given))
    far_factor = permute(factor, CORE)
    block = jnp.concatenate([kept, given], axis=1)

    gathered = [
        lax.optimization_barrier(
            [block[None, c * ROWS : (c + 1) * ROWS, DOFF[p] : DOFF[p] + DEPTH[p]] for p in range(3)]
        )
        for c in range(CHUNKS)
    ]
    for s in range(3):
        for c in range(CHUNKS):
            came = lax.optimization_barrier([permute(gathered[c][p], ROW_DIMS[(p + s) % 3]) for p in range(3)])
            gathered[c] = [jnp.concatenate([gathered[c][p], came[p]], axis=0) for p in range(3)]

    fho, flo = split(factor)
    norms = jnp.sum(factor * factor, axis=1)
    fhp, flp = split(far_factor)
    far_norms = jnp.sum(far_factor * far_factor, axis=1)
    factors = (fho, flo, fhp, flp)
    norms = norms + far_norms
    for d in range(3):
        norms = norms + permute(norms, COL_DIMS[d])

    inv = lax.rsqrt(norms)[None, :]
    floor_level = 0.25 * retention.astype(jnp.float32)
    cover = 0.25 * limit.astype(jnp.float32)
    onehot = (cell_entity[:, None] == jnp.arange(ENT, dtype=jnp.int32)[None, :]).astype(jnp.float32)
    every = (0, 1, 2)
    send_tbl, keep_tbl = tbl[0::2].reshape(36), tbl[1::2].reshape(36)
    results = []
    for c in range(CHUNKS):
        sent = mm(send_tbl, gathered[c], factors, every)
        came = lax.optimization_barrier([permute(sent[q], COL_DIMS[q]) for q in range(3)])
        kept = mm(keep_tbl, gathered[c], factors, every)
        second = lax.optimization_barrier([permute(kept[q][:2] + came[q][:2], COL_DIMS[(q + 1) % 3]) for q in range(3)])
        held = [kept[q][2:] + came[q][2:] + second[q] for q in range(3)]
        third = [permute(held[q][0], COL_DIMS[(q + 2) % 3]) for q in range(3)]
        mixed = jnp.concatenate([held[q][1] + third[q] for q in range(3)], axis=1)
        if c:
            mixed, _ = lax.optimization_barrier((mixed, sums))
        ground = scale[None, :] * jnp.exp(volatility[None, :] * (mixed * inv))
        ceded = jnp.minimum(jnp.maximum(ground - floor_level[None, :], 0.0), cover[None, :])
        net = ground - ceded
        sums = jnp.einsum("ksc,ce->kse", jnp.stack([net, ceded]), onehot, precision=lax.Precision.HIGH)
        parts = lax.all_to_all(sums, "row", split_axis=2, concat_axis=0, tiled=True)
        results.append(jnp.sum(parts.reshape(8, 2, ROWS, 128), axis=0))
    return jnp.concatenate(results, axis=1)


def solution(mesh):
    return jax.shard_map(
        step,
        mesh=mesh,
        in_specs=(
            P("row", "col"),
            P("row", "col"),
            P("row"),
            P("row"),
            P("row"),
            P("row"),
            P("row"),
        ),
        out_specs=P(None, "col", "row"),
        check_vma=False,
    )
```

```python
import functools

import jax
import jax.numpy as jnp
import numpy as np
from jax import lax
from jax.experimental import pallas as pl
from jax.experimental.pallas import tpu as pltpu
from jax.sharding import PartitionSpec as P


ENT = 1024
CHUNKS = 2
ROWS = 128 // CHUNKS
DEPTH = (768, 640, 640)
DOFF = (0, 768, 1408)
TILE = 256
COLS = (768, 768, 512)
COFF = (0, 768, 1536)
BOTH = ("row", "col")


def unflat(i):
    row, col = divmod(i, 16)
    return row // 4, row % 4, col // 4, col // 2 % 2, col % 2


def flat(yh, x, z, yl, core):
    return (yh * 4 + x) * 16 + z * 4 + yl * 2 + core


def perm(step):
    return [(i, flat(*step(*unflat(i)))) for i in range(128)]


CORE = perm(lambda yh, x, z, yl, c: (yh, x, z, yl, 1 - c))
ROW_DIMS = (
    perm(lambda yh, x, z, yl, c: (yh, x ^ 1, z, yl, c)),
    perm(lambda yh, x, z, yl, c: (yh, 3 - x, z, yl, c)),
    perm(lambda yh, x, z, yl, c: (1 - yh, x, z, yl, c)),
)
COL_DIMS = (
    perm(lambda yh, x, z, yl, c: (yh, x, z ^ 1, yl, c)),
    perm(lambda yh, x, z, yl, c: (yh, x, 3 - z, yl, c)),
    perm(lambda yh, x, z, yl, c: (yh, x, z, 1 - yl, c)),
)


def gray(v):
    return v ^ (v >> 1)


def ungray(v):
    return (v & 2) | ((v ^ (v >> 1)) & 1)


def place(e, p):
    return sum((e >> (p + s) % 3 & 1) << s for s in range(3))


def tables():
    out = np.zeros((128, 3, 8), np.int32)
    for i in range(128):
        yh, x, z, yl, _ = unflat(i)
        here_r, here_c = gray(x) | yh << 2, gray(z) | yl << 2
        for e in range(8):
            h = here_r ^ e
            source = (h >> 2) * 4 + ungray(h & 3)
            d = (gray(source >> 1) | (source & 1) << 2) ^ here_c
            for q in range(3):
                out[i, q, e] = 7 - sum((d >> (q + s) % 3 & 1) << 2 - s for s in range(3))
    return out.reshape(128, 24)


def permute(x, pairs):
    return lax.ppermute(x, BOTH, pairs)


def split(x):
    high = lax.reduce_precision(x, 8, 7)
    return high.astype(jnp.bfloat16), (x - high).astype(jnp.bfloat16)


STARTS = tuple(c // TILE for c in COFF)
SIZES = tuple(c // TILE for c in COLS)


def mm_kernel(tbl, *refs):
    first, last, (fho, flo, fhp, flp) = refs[:3], refs[3:6], refs[6:10]
    outs, both = refs[10:16], refs[16]
    m = 8 * ROWS
    t = pl.program_id(0)

    @pl.when(t == 0)
    def _():
        for e in range(8):
            for p in range(3):
                at = place(e, p)
                v = (last if at > 3 else first)[p][at & 3]
                h = v.astype(jnp.bfloat16)
                cols = pl.ds(DOFF[p], DEPTH[p])
                both[pl.ds(e * ROWS, ROWS), cols] = h
                both[pl.ds(m + e * ROWS, ROWS), cols] = (v - h.astype(jnp.float32)).astype(jnp.bfloat16)

    dot = functools.partial(
        lax.dot_general,
        dimension_numbers=(((1,), (1,)), ((), ())),
        preferred_element_type=jnp.float32,
    )
    own, far, high = pl.ds(0, 1024), pl.ds(1024, 1024), pl.ds(0, m)
    acc = dot(both[:, own], fho[...]) + dot(both[:, far], fhp[...])
    low = dot(both[high, own], flo[...]) + dot(both[high, far], flp[...])
    acc = acc[:m] + (acc[m:] + low)
    for q in range(3):

        @pl.when((t >= STARTS[q]) & (t < STARTS[q] + SIZES[q]))
        def _(q=q):
            for e in range(8):
                slot = tbl[q * 8 + e]
                v = acc[e * ROWS : (e + 1) * ROWS]

                @pl.when(slot < 4)
                def _():
                    outs[q][slot] = v

                @pl.when(slot > 3)
                def _():
                    outs[3 + q][slot - 4] = v


def mm(tbl, first, last, factors):
    whole = pl.BlockSpec(memory_space=pltpu.VMEM)
    outs = [
        pl.BlockSpec(
            (4, ROWS, TILE), lambda t, tb, q=q: (0, 0, jnp.clip(t - STARTS[q], 0, SIZES[q] - 1))
        )
        for q in range(3)
    ]
    res = pl.pallas_call(
        mm_kernel,
        out_shape=[jax.ShapeDtypeStruct((4, ROWS, COLS[q]), jnp.float32) for q in range(3)] * 2,
        grid_spec=pltpu.PrefetchScalarGridSpec(
            num_scalar_prefetch=1,
            grid=(2048 // TILE,),
            in_specs=[whole] * 6 + [pl.BlockSpec((TILE, 1024), lambda t, tb: (t, 0))] * 4,
            out_specs=outs * 2,
            scratch_shapes=[pltpu.VMEM((16 * ROWS, 2048), jnp.bfloat16)],
        ),
        cost_estimate=pl.CostEstimate(
            flops=2 * 3 * 8 * ROWS * 2048 * 2048,
            bytes_accessed=2 * 8 * ROWS * 2048 * 4 + 4 * 2048 * 2048,
            transcendentals=0,
        ),
        compiler_params=pltpu.CompilerParams(vmem_limit_bytes=28 * 2**20),
    )(tbl, *first, *last, *factors)
    return res[:3], res[3:]


def tail_kernel(*refs):
    pieces, (cells, out, both) = refs[:12], refs[12:]
    for q in range(3):
        cols = pl.ds(COFF[q], COLS[q])
        kept, came, second, third = pieces[q::3]
        mixed = kept[0] + came[0] + second[0] + third[0]
        inv, scale, vol, floor, cover = (cells[pl.ds(k, 1), cols] for k in range(5))
        ground = scale * jnp.exp(vol * (mixed * inv))
        ceded = jnp.minimum(jnp.maximum(ground - floor, 0.0), cover)
        for k, v in enumerate((ground - ceded, ceded)):
            h = v.astype(jnp.bfloat16)
            both[pl.ds(k * ROWS, ROWS), cols] = h
            both[pl.ds((2 + k) * ROWS, ROWS), cols] = (v - h.astype(jnp.float32)).astype(jnp.bfloat16)
    entity = cells[pl.ds(5, 1), :].astype(jnp.int32)
    for g in range(8):
        lines = lax.broadcasted_iota(jnp.int32, (128, 2048), 0) + g * 128
        onehot = jnp.where(lines == entity, 1.0, 0.0).astype(jnp.bfloat16)
        sums = lax.dot_general(
            both[...], onehot, (((1,), (1,)), ((), ())), preferred_element_type=jnp.float32
        )
        out[g] = sums[: 2 * ROWS] + sums[2 * ROWS :]


def tail(kept, came, second, third, cells):
    def block(at):
        return [pl.BlockSpec((1, ROWS, COLS[q]), lambda i: (at, 0, 0)) for q in range(3)]

    return pl.pallas_call(
        tail_kernel,
        out_shape=jax.ShapeDtypeStruct((8, 2 * ROWS, 128), jnp.float32),
        grid=(1,),
        in_specs=block(3) + block(3) + block(1) + block(0) + [pl.BlockSpec((6, 2048), lambda i: (0, 0))],
        out_specs=pl.BlockSpec((8, 2 * ROWS, 128), lambda i: (0, 0, 0)),
        scratch_shapes=[pltpu.VMEM((4 * ROWS, 2048), jnp.bfloat16)],
        cost_estimate=pl.CostEstimate(
            flops=2 * 4 * ROWS * 2048 * ENT, bytes_accessed=5 * ROWS * 2048 * 4, transcendentals=ROWS * 2048
        ),
        compiler_params=pltpu.CompilerParams(vmem_limit_bytes=16 * 2**20),
    )(*kept, *came, *second, *third, cells)


def step(normals, factor, cell_entity, scale, volatility, retention, limit):
    row, col = lax.axis_index("row"), lax.axis_index("col")
    core = col & 1
    tbl = lax.dynamic_index_in_dim(jnp.asarray(tables()), row * 16 + col, 0, False)

    given = permute(lax.dynamic_slice_in_dim(normals, (1 - core) * 128, 128, 0), CORE)
    kept = lax.dynamic_slice_in_dim(normals, core * 128, 128, 0)
    factor, given = lax.optimization_barrier((factor, given))
    far_factor = permute(factor, CORE)
    block = jnp.concatenate([kept, given], axis=1)

    gathered = [
        lax.optimization_barrier(
            [block[None, c * ROWS : (c + 1) * ROWS, DOFF[p] : DOFF[p] + DEPTH[p]] for p in range(3)]
        )
        for c in range(CHUNKS)
    ]
    last = []
    for s in range(3):
        for c in range(CHUNKS):
            came = lax.optimization_barrier([permute(gathered[c][p], ROW_DIMS[(p + s) % 3]) for p in range(3)])
            if s == 2:
                last.append(came)
                continue
            gathered[c] = [jnp.concatenate([gathered[c][p], came[p]], axis=0) for p in range(3)]

    fho, flo = split(factor)
    norms = jnp.sum(factor * factor, axis=1)
    fhp, flp = split(far_factor)
    far_norms = jnp.sum(far_factor * far_factor, axis=1)
    factors = (fho, flo, fhp, flp)
    norms = norms + far_norms
    for d in range(3):
        norms = norms + permute(norms, COL_DIMS[d])

    cells = jnp.stack(
        [
            lax.rsqrt(norms),
            scale,
            volatility,
            0.25 * retention.astype(jnp.float32),
            0.25 * limit.astype(jnp.float32),
            cell_entity.astype(jnp.float32),
        ]
    )
    results = []
    for c in range(CHUNKS):
        sent, kept = mm(tbl, gathered[c], last[c], factors)
        came = lax.optimization_barrier([permute(sent[q], COL_DIMS[q]) for q in range(3)])
        second = lax.optimization_barrier([permute(kept[q][:2] + came[q][:2], COL_DIMS[(q + 1) % 3]) for q in range(3)])
        third = lax.optimization_barrier(
            [permute(kept[q][2:3] + came[q][2:3] + second[q][:1], COL_DIMS[(q + 2) % 3]) for q in range(3)]
        )
        sums = tail(kept, came, second, third, cells)
        parts = lax.all_to_all(sums, "row", split_axis=0, concat_axis=0, tiled=True)
        results.append(jnp.sum(parts, axis=0).reshape(2, ROWS, 128))
    return jnp.concatenate(results, axis=1)


def solution(mesh):
    return jax.shard_map(
        step,
        mesh=mesh,
        in_specs=(
            P("row", "col"),
            P("row", "col"),
            P("row"),
            P("row"),
            P("row"),
            P("row"),
            P("row"),
        ),
        out_specs=P(None, "col", "row"),
        check_vma=False,
    )
```

```python
import functools

import jax
import jax.numpy as jnp
import numpy as np
from jax import lax
from jax.experimental import pallas as pl
from jax.experimental.pallas import tpu as pltpu
from jax.sharding import PartitionSpec as P


ENT = 1024
CHUNKS = 2
ROWS = 128 // CHUNKS
DEPTH = (768, 640, 640)
DOFF = (0, 768, 1408)
TILE = 256
COLS = (768, 768, 512)
COFF = (0, 768, 1536)
BOTH = ("row", "col")


def unflat(i):
    row, col = divmod(i, 16)
    return row // 4, row % 4, col // 4, col // 2 % 2, col % 2


def flat(yh, x, z, yl, core):
    return (yh * 4 + x) * 16 + z * 4 + yl * 2 + core


def perm(step):
    return [(i, flat(*step(*unflat(i)))) for i in range(128)]


CORE = perm(lambda yh, x, z, yl, c: (yh, x, z, yl, 1 - c))
ROW_DIMS = (
    perm(lambda yh, x, z, yl, c: (yh, x ^ 1, z, yl, c)),
    perm(lambda yh, x, z, yl, c: (yh, 3 - x, z, yl, c)),
    perm(lambda yh, x, z, yl, c: (1 - yh, x, z, yl, c)),
)
COL_DIMS = (
    perm(lambda yh, x, z, yl, c: (yh, x, z ^ 1, yl, c)),
    perm(lambda yh, x, z, yl, c: (yh, x, 3 - z, yl, c)),
    perm(lambda yh, x, z, yl, c: (yh, x, z, 1 - yl, c)),
)
ROW_XOR = [[(i, i ^ (k * 16)) for i in range(128)] for k in range(8)]


def gray(v):
    return v ^ (v >> 1)


def ungray(v):
    return (v & 2) | ((v ^ (v >> 1)) & 1)


def place(e, p):
    return sum((e >> (p + s) % 3 & 1) << s for s in range(3))


def tables():
    out = np.zeros((128, 3, 8), np.int32)
    for i in range(128):
        yh, x, z, yl, _ = unflat(i)
        here_r, here_c = gray(x) | yh << 2, gray(z) | yl << 2
        for e in range(8):
            h = here_r ^ e
            source = (h >> 2) * 4 + ungray(h & 3)
            d = (gray(source >> 1) | (source & 1) << 2) ^ here_c
            for q in range(3):
                out[i, q, 7 - sum((d >> (q + s) % 3 & 1) << 2 - s for s in range(3))] = e
    return out.reshape(128, 24)


def permute(x, pairs):
    return lax.ppermute(x, BOTH, pairs)


def split(x):
    high = lax.reduce_precision(x, 8, 7)
    return high.astype(jnp.bfloat16), (x - high).astype(jnp.bfloat16)


STARTS = tuple(c // TILE for c in COFF)
SIZES = tuple(c // TILE for c in COLS)


def mm_kernel(half, tbl, *refs):
    if half == 0:
        first, last, refs = refs[:3], refs[3:6], refs[6:]
    else:
        parts, refs = refs[0], refs[1:]
    (fho, flo, fhp, flp), outs, refs = refs[:4], refs[4:7], refs[7:]
    m = 4 * ROWS
    t = pl.program_id(0)
    if half == 0:
        parts, lhs = refs

        @pl.when(t == 0)
        def _():
            for e in range(8):
                for p in range(3):
                    at = place(e, p)
                    v = (last if at > 3 else first)[p][at & 3]
                    h = v.astype(jnp.bfloat16)
                    cols = pl.ds(DOFF[p], DEPTH[p])
                    parts[0, e, :, cols] = h
                    parts[1, e, :, cols] = (v - h.astype(jnp.float32)).astype(jnp.bfloat16)

    else:
        (lhs,) = refs
    for q in range(3):

        @pl.when(t == STARTS[q])
        def _(q=q):
            for i in range(4):
                e = tbl[q * 8 + half * 4 + i]
                for k in range(2):
                    lhs[pl.ds(k * m + i * ROWS, ROWS), :] = parts[k, e]

    dot = functools.partial(
        lax.dot_general,
        dimension_numbers=(((1,), (1,)), ((), ())),
        preferred_element_type=jnp.float32,
    )
    own, far, high = pl.ds(0, 1024), pl.ds(1024, 1024), pl.ds(0, m)
    rows = pl.ds(pl.multiple_of(t * TILE, TILE), TILE)
    acc = dot(lhs[:, own], fho[rows, :]) + dot(lhs[:, far], fhp[rows, :])
    low = dot(lhs[high, own], flo[rows, :]) + dot(lhs[high, far], flp[rows, :])
    acc = (acc[:m] + (acc[m:] + low)).reshape(4, ROWS, TILE)
    for q in range(3):

        @pl.when((t >= STARTS[q]) & (t < STARTS[q] + SIZES[q]))
        def _(q=q):
            outs[q][...] = acc


def mm(half, tbl, pieces, factors):
    whole = pl.BlockSpec(memory_space=pltpu.VMEM)
    outs = [
        pl.BlockSpec(
            (4, ROWS, TILE), lambda t, tb, q=q: (0, 0, jnp.clip(t - STARTS[q], 0, SIZES[q] - 1))
        )
        for q in range(3)
    ]
    shapes = [jax.ShapeDtypeStruct((4, ROWS, COLS[q]), jnp.float32) for q in range(3)]
    if half == 0:
        outs.append(whole)
        shapes.append(jax.ShapeDtypeStruct((2, 8, ROWS, 2048), jnp.bfloat16))
    res = pl.pallas_call(
        functools.partial(mm_kernel, half),
        out_shape=shapes,
        grid_spec=pltpu.PrefetchScalarGridSpec(
            num_scalar_prefetch=1,
            grid=(2048 // TILE,),
            in_specs=[whole] * (len(pieces) + 4),
            out_specs=outs,
            scratch_shapes=[pltpu.VMEM((8 * ROWS, 2048), jnp.bfloat16)],
        ),
        cost_estimate=pl.CostEstimate(
            flops=2 * 3 * 4 * ROWS * 2048 * 2048,
            bytes_accessed=2 * 4 * ROWS * 2048 * 4 + 4 * 2048 * 2048,
            transcendentals=0,
        ),
        compiler_params=pltpu.CompilerParams(vmem_limit_bytes=8 * 2**20),
    )(tbl, *pieces, *factors)
    return res[:3], res[3:]


def tail_kernel(row, *refs):
    pieces, cells, outs, both = refs[:6], refs[6], refs[7:15], refs[15]
    for q in range(3):
        cols = pl.ds(COFF[q], COLS[q])
        mixed = pieces[q][0] + pieces[3 + q][0]
        inv, scale, vol, floor, cover = (cells[pl.ds(k, 1), cols] for k in range(5))
        ground = scale * jnp.exp(vol * (mixed * inv))
        ceded = jnp.minimum(jnp.maximum(ground - floor, 0.0), cover)
        for k, v in enumerate((ground - ceded, ceded)):
            h = v.astype(jnp.bfloat16)
            both[pl.ds(k * ROWS, ROWS), cols] = h
            both[pl.ds((2 + k) * ROWS, ROWS), cols] = (v - h.astype(jnp.float32)).astype(jnp.bfloat16)
    entity = cells[pl.ds(5, 1), :].astype(jnp.int32)
    for k in range(8):
        lines = lax.broadcasted_iota(jnp.int32, (128, 2048), 0) + (row[0] ^ k) * 128
        onehot = jnp.where(lines == entity, 1.0, 0.0).astype(jnp.bfloat16)
        sums = lax.dot_general(
            both[...], onehot, (((1,), (1,)), ((), ())), preferred_element_type=jnp.float32
        )
        outs[k][...] = sums[: 2 * ROWS] + sums[2 * ROWS :]


def tail(row, held, third, cells):
    def at(shape):
        return pl.BlockSpec(shape, lambda i, r: (0,) * len(shape))

    return pl.pallas_call(
        tail_kernel,
        out_shape=[jax.ShapeDtypeStruct((2 * ROWS, 128), jnp.float32)] * 8,
        grid_spec=pltpu.PrefetchScalarGridSpec(
            num_scalar_prefetch=1,
            grid=(1,),
            in_specs=[at((1, ROWS, COLS[q])) for q in range(3)] * 2 + [at((6, 2048))],
            out_specs=[at((2 * ROWS, 128))] * 8,
            scratch_shapes=[pltpu.VMEM((4 * ROWS, 2048), jnp.bfloat16)],
        ),
        cost_estimate=pl.CostEstimate(
            flops=2 * 4 * ROWS * 2048 * ENT, bytes_accessed=5 * ROWS * 2048 * 4, transcendentals=ROWS * 2048
        ),
        compiler_params=pltpu.CompilerParams(vmem_limit_bytes=16 * 2**20),
    )(row.reshape(1), *held, *third, cells)


def step(normals, factor, cell_entity, scale, volatility, retention, limit):
    row, col = lax.axis_index("row"), lax.axis_index("col")
    core = col & 1
    tbl = lax.dynamic_index_in_dim(jnp.asarray(tables()), row * 16 + col, 0, False)

    given = permute(lax.dynamic_slice_in_dim(normals, (1 - core) * 128, 128, 0), CORE)
    kept = lax.dynamic_slice_in_dim(normals, core * 128, 128, 0)
    factor, given = lax.optimization_barrier((factor, given))
    far_factor = permute(factor, CORE)
    block = jnp.concatenate([kept[:, DEPTH[0] :], given], axis=1)
    gathered = [
        [
            kept[None, c * ROWS : (c + 1) * ROWS, : DEPTH[0]],
            block[None, c * ROWS : (c + 1) * ROWS, : DEPTH[1]],
            block[None, c * ROWS : (c + 1) * ROWS, DEPTH[1] :],
        ]
        for c in range(CHUNKS)
    ]
    last = []
    for s in range(3):
        for c in range(CHUNKS):
            came = lax.optimization_barrier([permute(gathered[c][p], ROW_DIMS[(p + s) % 3]) for p in range(3)])
            if s == 2:
                last.append(came)
                continue
            gathered[c] = [jnp.concatenate([gathered[c][p], came[p]], axis=0) for p in range(3)]

    fho, flo = split(factor)
    norms = jnp.sum(factor * factor, axis=1)
    fhp, flp = split(far_factor)
    far_norms = jnp.sum(far_factor * far_factor, axis=1)
    factors = (fho, flo, fhp, flp)
    norms = norms + far_norms
    for d in range(3):
        norms = norms + permute(norms, COL_DIMS[d])

    cells = jnp.stack(
        [
            lax.rsqrt(norms),
            scale,
            volatility,
            0.25 * retention.astype(jnp.float32),
            0.25 * limit.astype(jnp.float32),
            cell_entity.astype(jnp.float32),
        ]
    )
    results = []
    for c in range(CHUNKS):
        sent, parts = mm(0, tbl, (*gathered[c], *last[c]), factors)
        came = lax.optimization_barrier([permute(sent[q], COL_DIMS[q]) for q in range(3)])
        kept, _ = mm(1, tbl, parts, factors)
        second = lax.optimization_barrier([permute(kept[q][:2] + came[q][:2], COL_DIMS[(q + 1) % 3]) for q in range(3)])
        third = lax.optimization_barrier(
            [permute(kept[q][2:3] + came[q][2:3] + second[q][:1], COL_DIMS[(q + 2) % 3]) for q in range(3)]
        )
        held = [kept[q][3:] + came[q][3:] + second[q][1:] for q in range(3)]
        sums = tail(row, held, third, cells)
        total = sums[0]
        for k in range(1, 8):
            total = total + permute(sums[k], ROW_XOR[k])
        results.append(total.reshape(2, ROWS, 128))
    return jnp.concatenate(results, axis=1)


def solution(mesh):
    return jax.shard_map(
        step,
        mesh=mesh,
        in_specs=(
            P("row", "col"),
            P("row", "col"),
            P("row"),
            P("row"),
            P("row"),
            P("row"),
            P("row"),
        ),
        out_specs=P(None, "col", "row"),
        check_vma=False,
    )
```

```python
import functools

import jax
import jax.numpy as jnp
import numpy as np
from jax import lax
from jax.experimental import pallas as pl
from jax.experimental.pallas import tpu as pltpu
from jax.sharding import PartitionSpec as P


ENT = 1024
CHUNKS = 2
ROWS = 128 // CHUNKS
DEPTH = (768, 640, 640)
DOFF = (0, 768, 1408)
TILE = 256
COLS = (768, 768, 512)
COFF = (0, 768, 1536)
BOTH = ("row", "col")


def unflat(i):
    row, col = divmod(i, 16)
    return row // 4, row % 4, col // 4, col // 2 % 2, col % 2


def flat(yh, x, z, yl, core):
    return (yh * 4 + x) * 16 + z * 4 + yl * 2 + core


def perm(step):
    return [(i, flat(*step(*unflat(i)))) for i in range(128)]


CORE = perm(lambda yh, x, z, yl, c: (yh, x, z, yl, 1 - c))
ROW_DIMS = (
    perm(lambda yh, x, z, yl, c: (yh, x ^ 1, z, yl, c)),
    perm(lambda yh, x, z, yl, c: (yh, 3 - x, z, yl, c)),
    perm(lambda yh, x, z, yl, c: (1 - yh, x, z, yl, c)),
)
COL_DIMS = (
    perm(lambda yh, x, z, yl, c: (yh, x, z ^ 1, yl, c)),
    perm(lambda yh, x, z, yl, c: (yh, x, 3 - z, yl, c)),
    perm(lambda yh, x, z, yl, c: (yh, x, z, 1 - yl, c)),
)


def gray(v):
    return v ^ (v >> 1)


def ungray(v):
    return (v & 2) | ((v ^ (v >> 1)) & 1)


def place(e, p):
    return sum((e >> (p + s) % 3 & 1) << s for s in range(3))


def tables():
    out = np.zeros((128, 3, 8), np.int32)
    for i in range(128):
        yh, x, z, yl, _ = unflat(i)
        here_r, here_c = gray(x) | yh << 2, gray(z) | yl << 2
        for e in range(8):
            h = here_r ^ e
            source = (h >> 2) * 4 + ungray(h & 3)
            d = (gray(source >> 1) | (source & 1) << 2) ^ here_c
            for q in range(3):
                out[i, q, 7 - sum((d >> (q + s) % 3 & 1) << 2 - s for s in range(3))] = e
    return out.reshape(128, 24)


def permute(x, pairs):
    return lax.ppermute(x, BOTH, pairs)


def split(x):
    high = lax.reduce_precision(x, 8, 7)
    return high.astype(jnp.bfloat16), (x - high).astype(jnp.bfloat16)


STARTS = tuple(c // TILE for c in COFF)
SIZES = tuple(c // TILE for c in COLS)


def mm_kernel(half, tbl, *refs):
    if half == 0:
        first, last, refs = refs[:3], refs[3:6], refs[6:]
    else:
        parts, refs = refs[0], refs[1:]
    (fho, flo, fhp, flp), outs, refs = refs[:4], refs[4:7], refs[7:]
    m = 4 * ROWS
    t = pl.program_id(0)
    if half == 0:
        parts, lhs = refs

        @pl.when(t == 0)
        def _():
            for e in range(8):
                for p in range(3):
                    at = place(e, p)
                    v = (last if at > 3 else first)[p][at & 3]
                    h = v.astype(jnp.bfloat16)
                    cols = pl.ds(DOFF[p], DEPTH[p])
                    parts[0, e, :, cols] = h
                    parts[1, e, :, cols] = (v - h.astype(jnp.float32)).astype(jnp.bfloat16)

    else:
        (lhs,) = refs
    for q in range(3):

        @pl.when(t == STARTS[q])
        def _(q=q):
            for i in range(4):
                e = tbl[q * 8 + half * 4 + i]
                for k in range(2):
                    lhs[pl.ds(k * m + i * ROWS, ROWS), :] = parts[k, e]

    dot = functools.partial(
        lax.dot_general,
        dimension_numbers=(((1,), (1,)), ((), ())),
        preferred_element_type=jnp.float32,
    )
    own, far, high = pl.ds(0, 1024), pl.ds(1024, 1024), pl.ds(0, m)
    rows = pl.ds(pl.multiple_of(t * TILE, TILE), TILE)
    acc = dot(lhs[:, own], fho[rows, :]) + dot(lhs[:, far], fhp[rows, :])
    low = dot(lhs[high, own], flo[rows, :]) + dot(lhs[high, far], flp[rows, :])
    acc = (acc[:m] + (acc[m:] + low)).reshape(4, ROWS, TILE)
    for q in range(3):

        @pl.when((t >= STARTS[q]) & (t < STARTS[q] + SIZES[q]))
        def _(q=q):
            outs[q][...] = acc


def mm(half, tbl, pieces, factors):
    whole = pl.BlockSpec(memory_space=pltpu.VMEM)
    outs = [
        pl.BlockSpec(
            (4, ROWS, TILE), lambda t, tb, q=q: (0, 0, jnp.clip(t - STARTS[q], 0, SIZES[q] - 1))
        )
        for q in range(3)
    ]
    shapes = [jax.ShapeDtypeStruct((4, ROWS, COLS[q]), jnp.float32) for q in range(3)]
    if half == 0:
        outs.append(whole)
        shapes.append(jax.ShapeDtypeStruct((2, 8, ROWS, 2048), jnp.bfloat16))
    res = pl.pallas_call(
        functools.partial(mm_kernel, half),
        out_shape=shapes,
        grid_spec=pltpu.PrefetchScalarGridSpec(
            num_scalar_prefetch=1,
            grid=(2048 // TILE,),
            in_specs=[whole] * (len(pieces) + 4),
            out_specs=outs,
            scratch_shapes=[pltpu.VMEM((8 * ROWS, 2048), jnp.bfloat16)],
        ),
        cost_estimate=pl.CostEstimate(
            flops=2 * 3 * 4 * ROWS * 2048 * 2048,
            bytes_accessed=2 * 4 * ROWS * 2048 * 4 + 4 * 2048 * 2048,
            transcendentals=0,
        ),
        compiler_params=pltpu.CompilerParams(vmem_limit_bytes=8 * 2**20),
    )(tbl, *pieces, *factors)
    return res[:3], res[3:]


def tail_kernel(*refs):
    pieces, cells, out, both = refs[:6], refs[6], refs[-2], refs[-1]
    for q in range(3):
        cols = pl.ds(COFF[q], COLS[q])
        mixed = pieces[q][0] + pieces[3 + q][0]
        inv, scale, vol, floor, cover = (cells[pl.ds(k, 1), cols] for k in range(5))
        ground = scale * jnp.exp(vol * (mixed * inv))
        ceded = jnp.minimum(jnp.maximum(ground - floor, 0.0), cover)
        for k, v in enumerate((ground - ceded, ceded)):
            h = v.astype(jnp.bfloat16)
            both[pl.ds(k * ROWS, ROWS), cols] = h
            both[pl.ds((2 + k) * ROWS, ROWS), cols] = (v - h.astype(jnp.float32)).astype(jnp.bfloat16)
    entity = cells[pl.ds(5, 1), :].astype(jnp.int32)
    before = len(refs) == 10
    for g in range(8):
        lines = lax.broadcasted_iota(jnp.int32, (128, 2048), 0) + g * 128
        onehot = jnp.where(lines == entity, 1.0, 0.0).astype(jnp.bfloat16)
        sums = lax.dot_general(
            both[...], onehot, (((1,), (1,)), ((), ())), preferred_element_type=jnp.float32
        )
        sums = sums[: 2 * ROWS] + sums[2 * ROWS :]
        if before:
            out[g, pl.ds(0, 2 * ROWS), :] = refs[7][g]
            out[g, pl.ds(2 * ROWS, 2 * ROWS), :] = sums
        else:
            out[g] = sums


def tail(held, third, cells, before):
    def at(shape):
        return pl.BlockSpec(shape, lambda i: (0,) * len(shape))

    rows = 2 * ROWS * (1 + len(before))
    return pl.pallas_call(
        tail_kernel,
        out_shape=jax.ShapeDtypeStruct((8, rows, 128), jnp.float32),
        grid=(1,),
        in_specs=[at((1, ROWS, COLS[q])) for q in range(3)] * 2
        + [at((6, 2048))]
        + [at((8, 2 * ROWS, 128))] * len(before),
        out_specs=at((8, rows, 128)),
        scratch_shapes=[pltpu.VMEM((4 * ROWS, 2048), jnp.bfloat16)],
        cost_estimate=pl.CostEstimate(
            flops=2 * 4 * ROWS * 2048 * ENT, bytes_accessed=5 * ROWS * 2048 * 4, transcendentals=ROWS * 2048
        ),
        compiler_params=pltpu.CompilerParams(vmem_limit_bytes=16 * 2**20),
    )(*held, *third, cells, *before)


def step(normals, factor, cell_entity, scale, volatility, retention, limit):
    row, col = lax.axis_index("row"), lax.axis_index("col")
    core = col & 1
    tbl = lax.dynamic_index_in_dim(jnp.asarray(tables()), row * 16 + col, 0, False)

    given = permute(lax.dynamic_slice_in_dim(normals, (1 - core) * 128, 128, 0), CORE)
    kept = lax.dynamic_slice_in_dim(normals, core * 128, 128, 0)
    factor, given = lax.optimization_barrier((factor, given))
    far_factor = permute(factor, CORE)
    block = jnp.concatenate([kept[:, DEPTH[0] :], given], axis=1)
    gathered = [
        [
            kept[None, c * ROWS : (c + 1) * ROWS, : DEPTH[0]],
            block[None, c * ROWS : (c + 1) * ROWS, : DEPTH[1]],
            block[None, c * ROWS : (c + 1) * ROWS, DEPTH[1] :],
        ]
        for c in range(CHUNKS)
    ]
    last = []
    for s in range(3):
        for c in range(CHUNKS):
            came = lax.optimization_barrier([permute(gathered[c][p], ROW_DIMS[(p + s) % 3]) for p in range(3)])
            if s == 2:
                last.append(came)
                continue
            gathered[c] = [jnp.concatenate([gathered[c][p], came[p]], axis=0) for p in range(3)]

    fho, flo = split(factor)
    norms = jnp.sum(factor * factor, axis=1)
    fhp, flp = split(far_factor)
    far_norms = jnp.sum(far_factor * far_factor, axis=1)
    factors = (fho, flo, fhp, flp)
    norms = norms + far_norms
    for d in range(3):
        norms = norms + permute(norms, COL_DIMS[d])

    cells = jnp.stack(
        [
            lax.rsqrt(norms),
            scale,
            volatility,
            0.25 * retention.astype(jnp.float32),
            0.25 * limit.astype(jnp.float32),
            cell_entity.astype(jnp.float32),
        ]
    )
    sums = ()
    for c in range(CHUNKS):
        sent, parts = mm(0, tbl, (*gathered[c], *last[c]), factors)
        came = lax.optimization_barrier([permute(sent[q], COL_DIMS[q]) for q in range(3)])
        kept, _ = mm(1, tbl, parts, factors)
        second = lax.optimization_barrier([permute(kept[q][:2] + came[q][:2], COL_DIMS[(q + 1) % 3]) for q in range(3)])
        third = lax.optimization_barrier(
            [permute(kept[q][2:3] + came[q][2:3] + second[q][:1], COL_DIMS[(q + 2) % 3]) for q in range(3)]
        )
        held = [kept[q][3:] + came[q][3:] + second[q][1:] for q in range(3)]
        sums = (tail(held, third, cells, sums),)
    parts = lax.all_to_all(sums[0], "row", split_axis=0, concat_axis=0, tiled=True)
    total = jnp.sum(parts, axis=0).reshape(CHUNKS, 2, ROWS, 128)
    return jnp.swapaxes(total, 0, 1).reshape(2, 128, 128)


def solution(mesh):
    return jax.shard_map(
        step,
        mesh=mesh,
        in_specs=(
            P("row", "col"),
            P("row", "col"),
            P("row"),
            P("row"),
            P("row"),
            P("row"),
            P("row"),
        ),
        out_specs=P(None, "col", "row"),
        check_vma=False,
    )
```

```python
import functools

import jax
import jax.numpy as jnp
import numpy as np
from jax import lax
from jax.experimental import pallas as pl
from jax.experimental.pallas import tpu as pltpu
from jax.sharding import PartitionSpec as P


ENT = 1024
CHUNKS = 2
ROWS = 128 // CHUNKS
DEPTH = (768, 640, 640)
DOFF = (0, 768, 1408)
TILE = 256
COLS = (768, 768, 512)
COFF = (0, 768, 1536)
BOTH = ("row", "col")


def unflat(i):
    row, col = divmod(i, 16)
    return row // 4, row % 4, col // 4, col // 2 % 2, col % 2


def flat(yh, x, z, yl, core):
    return (yh * 4 + x) * 16 + z * 4 + yl * 2 + core


def perm(step):
    return [(i, flat(*step(*unflat(i)))) for i in range(128)]


CORE = perm(lambda yh, x, z, yl, c: (yh, x, z, yl, 1 - c))
ROW_DIMS = (
    perm(lambda yh, x, z, yl, c: (yh, x ^ 1, z, yl, c)),
    perm(lambda yh, x, z, yl, c: (yh, 3 - x, z, yl, c)),
    perm(lambda yh, x, z, yl, c: (1 - yh, x, z, yl, c)),
)
COL_DIMS = (
    perm(lambda yh, x, z, yl, c: (yh, x, z ^ 1, yl, c)),
    perm(lambda yh, x, z, yl, c: (yh, x, 3 - z, yl, c)),
    perm(lambda yh, x, z, yl, c: (yh, x, z, 1 - yl, c)),
)


def gray(v):
    return v ^ (v >> 1)


def ungray(v):
    return (v & 2) | ((v ^ (v >> 1)) & 1)


def place(e, p):
    return sum((e >> (p + s) % 3 & 1) << s for s in range(3))


def tables():
    out = np.zeros((128, 3, 8), np.int32)
    for i in range(128):
        yh, x, z, yl, _ = unflat(i)
        here_r, here_c = gray(x) | yh << 2, gray(z) | yl << 2
        for e in range(8):
            h = here_r ^ e
            source = (h >> 2) * 4 + ungray(h & 3)
            d = (gray(source >> 1) | (source & 1) << 2) ^ here_c
            for q in range(3):
                out[i, q, 7 - sum((d >> (q + s) % 3 & 1) << 2 - s for s in range(3))] = e
    return out.reshape(128, 24)


def permute(x, pairs):
    return lax.ppermute(x, BOTH, pairs)


def split(x):
    high = lax.reduce_precision(x, 8, 7)
    return high.astype(jnp.bfloat16), (x - high).astype(jnp.bfloat16)


STARTS = tuple(c // TILE for c in COFF)
SIZES = tuple(c // TILE for c in COLS)


def mm_kernel(half, tbl, *refs):
    if half == 0:
        first, last, refs = refs[:3], refs[3:6], refs[6:]
    else:
        parts, refs = refs[0], refs[1:]
    (fho, flo, fhp, flp), outs, refs = refs[:4], refs[4:7], refs[7:]
    m = 4 * ROWS
    t = pl.program_id(0)
    if half == 0:
        parts, lhs = refs

        @pl.when(t == 0)
        def _():
            for e in range(8):
                for p in range(3):
                    at = place(e, p)
                    v = (last if at > 3 else first)[p][at & 3]
                    h = v.astype(jnp.bfloat16)
                    cols = pl.ds(DOFF[p], DEPTH[p])
                    parts[0, e, :, cols] = h
                    parts[1, e, :, cols] = (v - h.astype(jnp.float32)).astype(jnp.bfloat16)

    else:
        (lhs,) = refs
    for q in range(3):

        @pl.when(t == STARTS[q])
        def _(q=q):
            for i in range(4):
                e = tbl[q * 8 + half * 4 + i]
                for k in range(2):
                    lhs[pl.ds(k * m + i * ROWS, ROWS), :] = parts[k, e]

    dot = functools.partial(
        lax.dot_general,
        dimension_numbers=(((1,), (1,)), ((), ())),
        preferred_element_type=jnp.float32,
    )
    own, far, high = pl.ds(0, 1024), pl.ds(1024, 1024), pl.ds(0, m)
    rows = pl.ds(pl.multiple_of(t * TILE, TILE), TILE)
    acc = dot(lhs[:, own], fho[rows, :]) + dot(lhs[:, far], fhp[rows, :])
    low = dot(lhs[high, own], flo[rows, :]) + dot(lhs[high, far], flp[rows, :])
    acc = (acc[:m] + (acc[m:] + low)).reshape(4, ROWS, TILE)
    for q in range(3):

        @pl.when((t >= STARTS[q]) & (t < STARTS[q] + SIZES[q]))
        def _(q=q):
            outs[q][...] = acc


def mm(half, tbl, pieces, factors):
    whole = pl.BlockSpec(memory_space=pltpu.VMEM)
    outs = [
        pl.BlockSpec(
            (4, ROWS, TILE), lambda t, tb, q=q: (0, 0, jnp.clip(t - STARTS[q], 0, SIZES[q] - 1))
        )
        for q in range(3)
    ]
    shapes = [jax.ShapeDtypeStruct((4, ROWS, COLS[q]), jnp.float32) for q in range(3)]
    if half == 0:
        outs.append(whole)
        shapes.append(jax.ShapeDtypeStruct((2, 8, ROWS, 2048), jnp.bfloat16))
    res = pl.pallas_call(
        functools.partial(mm_kernel, half),
        out_shape=shapes,
        grid_spec=pltpu.PrefetchScalarGridSpec(
            num_scalar_prefetch=1,
            grid=(2048 // TILE,),
            in_specs=[whole] * (len(pieces) + 4),
            out_specs=outs,
            scratch_shapes=[pltpu.VMEM((8 * ROWS, 2048), jnp.bfloat16)],
        ),
        cost_estimate=pl.CostEstimate(
            flops=2 * 3 * 4 * ROWS * 2048 * 2048,
            bytes_accessed=2 * 4 * ROWS * 2048 * 4 + 4 * 2048 * 2048,
            transcendentals=0,
        ),
        compiler_params=pltpu.CompilerParams(vmem_limit_bytes=8 * 2**20),
    )(tbl, *pieces, *factors)
    return res[:3], res[3:]


def tail_kernel(*refs):
    pieces, cells, out, both = refs[:6], refs[6], refs[-2], refs[-1]
    for q in range(3):
        cols = pl.ds(COFF[q], COLS[q])
        mixed = pieces[q][0] + pieces[3 + q][0]
        inv, scale, vol, floor, cover = (cells[pl.ds(k, 1), cols] for k in range(5))
        ground = scale * jnp.exp(vol * (mixed * inv))
        ceded = jnp.minimum(jnp.maximum(ground - floor, 0.0), cover)
        for k, v in enumerate((ground - ceded, ceded)):
            h = v.astype(jnp.bfloat16)
            both[pl.ds(k * ROWS, ROWS), cols] = h
            both[pl.ds((2 + k) * ROWS, ROWS), cols] = (v - h.astype(jnp.float32)).astype(jnp.bfloat16)
    entity = cells[pl.ds(5, 1), :].astype(jnp.int32)
    before = len(refs) == 10
    for g in range(8):
        lines = lax.broadcasted_iota(jnp.int32, (128, 2048), 0) + g * 128
        onehot = jnp.where(lines == entity, 1.0, 0.0).astype(jnp.bfloat16)
        sums = lax.dot_general(
            both[...], onehot, (((1,), (1,)), ((), ())), preferred_element_type=jnp.float32
        )
        sums = sums[: 2 * ROWS] + sums[2 * ROWS :]
        if before:
            out[g, pl.ds(0, 2 * ROWS), :] = refs[7][g]
            out[g, pl.ds(2 * ROWS, 2 * ROWS), :] = sums
        else:
            out[g] = sums


def tail(held, third, cells, before):
    def at(shape):
        return pl.BlockSpec(shape, lambda i: (0,) * len(shape))

    rows = 2 * ROWS * (1 + len(before))
    return pl.pallas_call(
        tail_kernel,
        out_shape=jax.ShapeDtypeStruct((8, rows, 128), jnp.float32),
        grid=(1,),
        in_specs=[at((1, ROWS, COLS[q])) for q in range(3)] * 2
        + [at((6, 2048))]
        + [at((8, 2 * ROWS, 128))] * len(before),
        out_specs=at((8, rows, 128)),
        scratch_shapes=[pltpu.VMEM((4 * ROWS, 2048), jnp.bfloat16)],
        cost_estimate=pl.CostEstimate(
            flops=2 * 4 * ROWS * 2048 * ENT, bytes_accessed=5 * ROWS * 2048 * 4, transcendentals=ROWS * 2048
        ),
        compiler_params=pltpu.CompilerParams(vmem_limit_bytes=16 * 2**20),
    )(*held, *third, cells, *before)


def step(normals, factor, cell_entity, scale, volatility, retention, limit):
    row, col = lax.axis_index("row"), lax.axis_index("col")
    core = col & 1
    tbl = lax.dynamic_index_in_dim(jnp.asarray(tables()), row * 16 + col, 0, False)

    given = permute(lax.dynamic_slice_in_dim(normals, (1 - core) * 128, 128, 0), CORE)
    kept = lax.dynamic_slice_in_dim(normals, core * 128, 128, 0)
    factor, given = lax.optimization_barrier((factor, given))
    far_factor = permute(factor, CORE)
    block = jnp.concatenate([kept[:, DEPTH[0] :], given], axis=1)
    first = [kept[None, c * ROWS : (c + 1) * ROWS, : DEPTH[0]] for c in range(CHUNKS)]
    gathered = [
        [
            first[c],
            block[None, c * ROWS : (c + 1) * ROWS, : DEPTH[1]],
            block[None, c * ROWS : (c + 1) * ROWS, DEPTH[1] :],
        ]
        for c in range(CHUNKS)
    ]
    last = []
    for s in range(3):
        for c in range(CHUNKS):
            came = lax.optimization_barrier(
                [permute(gathered[c][p], ROW_DIMS[(p + s) % 3]) for p in range(3)]
            )
            if s == 2:
                last.append(came)
                continue
            gathered[c] = [jnp.concatenate([gathered[c][p], came[p]], axis=0) for p in range(3)]

    fho, flo = split(factor)
    norms = jnp.sum(factor * factor, axis=1)
    fhp, flp = split(far_factor)
    far_norms = jnp.sum(far_factor * far_factor, axis=1)
    factors = (fho, flo, fhp, flp)
    norms = norms + far_norms
    for d in range(3):
        norms = norms + permute(norms, COL_DIMS[d])

    cells = jnp.stack(
        [
            lax.rsqrt(norms),
            scale,
            volatility,
            0.25 * retention.astype(jnp.float32),
            0.25 * limit.astype(jnp.float32),
            cell_entity.astype(jnp.float32),
        ]
    )
    sums = ()
    for c in range(CHUNKS):
        sent, parts = mm(0, tbl, (*gathered[c], *last[c]), factors)
        came = lax.optimization_barrier([permute(sent[q], COL_DIMS[q]) for q in range(3)])
        kept, _ = mm(1, tbl, parts, factors)
        passed = [kept[q][:2] + came[q][:2] for q in range(3)]
        second = lax.optimization_barrier(
            [permute(passed[q], COL_DIMS[(q + 1) % 3]) for q in range(3)]
        )
        passed = [kept[q][2:3] + came[q][2:3] + second[q][:1] for q in range(3)]
        third = lax.optimization_barrier(
            [permute(passed[q], COL_DIMS[(q + 2) % 3]) for q in range(3)]
        )
        held = [kept[q][3:] + came[q][3:] + second[q][1:] for q in range(3)]
        sums = (tail(held, third, cells, sums),)
    parts = lax.all_to_all(sums[0], "row", split_axis=0, concat_axis=0, tiled=True)
    total = jnp.sum(parts, axis=0).reshape(CHUNKS, 2, ROWS, 128)
    return jnp.swapaxes(total, 0, 1).reshape(2, 128, 128)


def solution(mesh):
    return jax.shard_map(
        step,
        mesh=mesh,
        in_specs=(
            P("row", "col"),
            P("row", "col"),
            P("row"),
            P("row"),
            P("row"),
            P("row"),
            P("row"),
        ),
        out_specs=P(None, "col", "row"),
        check_vma=False,
    )
```

```python
import functools

import jax
import jax.numpy as jnp
import numpy as np
from jax import lax
from jax.experimental import pallas as pl
from jax.experimental.pallas import tpu as pltpu
from jax.sharding import PartitionSpec as P


ENT = 1024
CHUNKS = 2
ROWS = 128 // CHUNKS
DEPTH = (768, 640, 640)
DOFF = (0, 768, 1408)
TILE = 256
LIFT = 256.0
COLS = (768, 768, 512)
COFF = (0, 768, 1536)
BOTH = ("row", "col")


def unflat(i):
    row, col = divmod(i, 16)
    return row // 4, row % 4, col // 4, col // 2 % 2, col % 2


def flat(yh, x, z, yl, core):
    return (yh * 4 + x) * 16 + z * 4 + yl * 2 + core


def perm(step):
    return [(i, flat(*step(*unflat(i)))) for i in range(128)]


CORE = perm(lambda yh, x, z, yl, c: (yh, x, z, yl, 1 - c))
ROW_DIMS = (
    perm(lambda yh, x, z, yl, c: (yh, x ^ 1, z, yl, c)),
    perm(lambda yh, x, z, yl, c: (yh, 3 - x, z, yl, c)),
    perm(lambda yh, x, z, yl, c: (1 - yh, x, z, yl, c)),
)
COL_DIMS = (
    perm(lambda yh, x, z, yl, c: (yh, x, z ^ 1, yl, c)),
    perm(lambda yh, x, z, yl, c: (yh, x, 3 - z, yl, c)),
    perm(lambda yh, x, z, yl, c: (yh, x, z, 1 - yl, c)),
)


def gray(v):
    return v ^ (v >> 1)


def ungray(v):
    return (v & 2) | ((v ^ (v >> 1)) & 1)


def place(e, p):
    return sum((e >> (p + s) % 3 & 1) << s for s in range(3))


def tables():
    out = np.zeros((128, 3, 8), np.int32)
    for i in range(128):
        yh, x, z, yl, _ = unflat(i)
        here_r, here_c = gray(x) | yh << 2, gray(z) | yl << 2
        for e in range(8):
            h = here_r ^ e
            source = (h >> 2) * 4 + ungray(h & 3)
            d = (gray(source >> 1) | (source & 1) << 2) ^ here_c
            for q in range(3):
                out[i, q, 7 - sum((d >> (q + s) % 3 & 1) << 2 - s for s in range(3))] = e
    return out.reshape(128, 24)


def permute(x, pairs):
    return lax.ppermute(x, BOTH, pairs)


def to_f8(x):
    return jnp.clip(x, -440.0, 440.0).astype(jnp.float8_e4m3fn)


def split(x, level):
    high = lax.reduce_precision(x, 8, 7)
    return (
        high.astype(jnp.bfloat16),
        to_f8(high * level[:, None]),
        to_f8((x - high) * (level * LIFT)[:, None]),
    )


STARTS = tuple(c // TILE for c in COFF)
SIZES = tuple(c // TILE for c in COLS)


def mm_kernel(half, tbl, *refs):
    if half == 0:
        first, last, refs = refs[:3], refs[3:6], refs[6:]
    else:
        (high, cross), refs = refs[:2], refs[2:]
    (own16, own8, own_rest, far16, far8, far_rest, level), refs = refs[:7], refs[7:]
    outs, refs = refs[:3], refs[3:]
    t = pl.program_id(0)
    if half == 0:
        high, cross, lhs16, lhs8 = refs

        @pl.when(t == 0)
        def _():
            for e in range(8):
                for p in range(3):
                    at = place(e, p)
                    v = (last if at > 3 else first)[p][at & 3]
                    h = v.astype(jnp.bfloat16)
                    cols = pl.ds(DOFF[p], DEPTH[p])
                    high[e, :, cols] = h
                    cross[0, e, :, cols] = v.astype(jnp.float8_e4m3fn)
                    rest = (v - h.astype(jnp.float32)) * LIFT
                    cross[1, e, :, cols] = rest.astype(jnp.float8_e4m3fn)

    else:
        lhs16, lhs8 = refs
    for q in range(3):

        @pl.when(t == STARTS[q])
        def _(q=q):
            for i in range(4):
                e = tbl[q * 8 + half * 4 + i]
                at = pl.ds(i * ROWS, ROWS)
                lhs16[at, :] = high[e]
                for k in range(2):
                    lhs8[k, at, :] = cross[k, e]

    dot = functools.partial(
        lax.dot_general,
        dimension_numbers=(((1,), (1,)), ((), ())),
        preferred_element_type=jnp.float32,
    )
    own, far = pl.ds(0, 1024), pl.ds(1024, 1024)
    rows = pl.ds(pl.multiple_of(t * TILE, TILE), TILE)
    acc = dot(lhs16[:, own], own16[rows, :]) + dot(lhs16[:, far], far16[rows, :])
    low = dot(lhs8[0, :, own], own_rest[rows, :]) + dot(lhs8[0, :, far], far_rest[rows, :])
    low += dot(lhs8[1, :, own], own8[rows, :]) + dot(lhs8[1, :, far], far8[rows, :])
    acc = (acc + low * level[...]).reshape(4, ROWS, TILE)
    for q in range(3):

        @pl.when((t >= STARTS[q]) & (t < STARTS[q] + SIZES[q]))
        def _(q=q):
            outs[q][...] = acc


def mm(half, tbl, pieces, factors):
    whole = pl.BlockSpec(memory_space=pltpu.VMEM)
    outs = [
        pl.BlockSpec(
            (4, ROWS, TILE), lambda t, tb, q=q: (0, 0, jnp.clip(t - STARTS[q], 0, SIZES[q] - 1))
        )
        for q in range(3)
    ]
    shapes = [jax.ShapeDtypeStruct((4, ROWS, COLS[q]), jnp.float32) for q in range(3)]
    if half == 0:
        outs += [whole] * 2
        shapes += [
            jax.ShapeDtypeStruct((8, ROWS, 2048), jnp.bfloat16),
            jax.ShapeDtypeStruct((2, 8, ROWS, 2048), jnp.float8_e4m3fn),
        ]
    res = pl.pallas_call(
        functools.partial(mm_kernel, half),
        out_shape=shapes,
        grid_spec=pltpu.PrefetchScalarGridSpec(
            num_scalar_prefetch=1,
            grid=(2048 // TILE,),
            in_specs=[whole] * (len(pieces) + 6) + [pl.BlockSpec((1, TILE), lambda t, tb: (0, t))],
            out_specs=outs,
            scratch_shapes=[
                pltpu.VMEM((4 * ROWS, 2048), jnp.bfloat16),
                pltpu.VMEM((2, 4 * ROWS, 2048), jnp.float8_e4m3fn),
            ],
        ),
        cost_estimate=pl.CostEstimate(
            flops=2 * 2 * 4 * ROWS * 2048 * 2048,
            bytes_accessed=2 * 4 * ROWS * 2048 * 4 + 4 * 2048 * 2048,
            transcendentals=0,
        ),
        compiler_params=pltpu.CompilerParams(vmem_limit_bytes=8 * 2**20),
    )(tbl, *pieces, *factors)
    return res[:3], res[3:]


def tail_kernel(*refs):
    pieces, cells, out, both = refs[:6], refs[6], refs[-2], refs[-1]
    for q in range(3):
        cols = pl.ds(COFF[q], COLS[q])
        mixed = pieces[q][0] + pieces[3 + q][0]
        inv, scale, vol, floor, cover = (cells[pl.ds(k, 1), cols] for k in range(5))
        ground = scale * jnp.exp(vol * (mixed * inv))
        ceded = jnp.minimum(jnp.maximum(ground - floor, 0.0), cover)
        for k, v in enumerate((ground - ceded, ceded)):
            h = v.astype(jnp.bfloat16)
            both[pl.ds(k * ROWS, ROWS), cols] = h
            both[pl.ds((2 + k) * ROWS, ROWS), cols] = (v - h.astype(jnp.float32)).astype(jnp.bfloat16)
    entity = cells[pl.ds(5, 1), :].astype(jnp.int32)
    before = len(refs) == 10
    for g in range(8):
        lines = lax.broadcasted_iota(jnp.int32, (128, 2048), 0) + g * 128
        onehot = jnp.where(lines == entity, 1.0, 0.0).astype(jnp.bfloat16)
        sums = lax.dot_general(
            both[...], onehot, (((1,), (1,)), ((), ())), preferred_element_type=jnp.float32
        )
        sums = sums[: 2 * ROWS] + sums[2 * ROWS :]
        if before:
            out[g, pl.ds(0, 2 * ROWS), :] = refs[7][g]
            out[g, pl.ds(2 * ROWS, 2 * ROWS), :] = sums
        else:
            out[g] = sums


def tail(held, third, cells, before):
    def at(shape):
        return pl.BlockSpec(shape, lambda i: (0,) * len(shape))

    rows = 2 * ROWS * (1 + len(before))
    return pl.pallas_call(
        tail_kernel,
        out_shape=jax.ShapeDtypeStruct((8, rows, 128), jnp.float32),
        grid=(1,),
        in_specs=[at((1, ROWS, COLS[q])) for q in range(3)] * 2
        + [at((6, 2048))]
        + [at((8, 2 * ROWS, 128))] * len(before),
        out_specs=at((8, rows, 128)),
        scratch_shapes=[pltpu.VMEM((4 * ROWS, 2048), jnp.bfloat16)],
        cost_estimate=pl.CostEstimate(
            flops=2 * 4 * ROWS * 2048 * ENT, bytes_accessed=5 * ROWS * 2048 * 4, transcendentals=ROWS * 2048
        ),
        compiler_params=pltpu.CompilerParams(vmem_limit_bytes=16 * 2**20),
    )(*held, *third, cells, *before)


def step(normals, factor, cell_entity, scale, volatility, retention, limit):
    row, col = lax.axis_index("row"), lax.axis_index("col")
    core = col & 1
    tbl = lax.dynamic_index_in_dim(jnp.asarray(tables()), row * 16 + col, 0, False)

    given = permute(lax.dynamic_slice_in_dim(normals, (1 - core) * 128, 128, 0), CORE)
    kept = lax.dynamic_slice_in_dim(normals, core * 128, 128, 0)
    factor, given = lax.optimization_barrier((factor, given))
    far_factor = permute(factor, CORE)
    block = jnp.concatenate([kept[:, DEPTH[0] :], given], axis=1)
    first = [kept[None, c * ROWS : (c + 1) * ROWS, : DEPTH[0]] for c in range(CHUNKS)]
    gathered = [
        [
            first[c],
            block[None, c * ROWS : (c + 1) * ROWS, : DEPTH[1]],
            block[None, c * ROWS : (c + 1) * ROWS, DEPTH[1] :],
        ]
        for c in range(CHUNKS)
    ]
    last = []
    for s in range(3):
        for c in range(CHUNKS):
            came = lax.optimization_barrier(
                [permute(gathered[c][p], ROW_DIMS[(p + s) % 3]) for p in range(3)]
            )
            if s == 2:
                last.append(came)
                continue
            gathered[c] = [jnp.concatenate([gathered[c][p], came[p]], axis=0) for p in range(3)]

    norms = jnp.sum(factor * factor, axis=1)
    norms = norms + permute(norms, CORE)
    level = 128.0 * lax.rsqrt(jnp.clip(norms, 1e-30, 1e38))
    level, unlevel, norms = lax.optimization_barrier((level, 1.0 / (level * LIFT), norms))
    own = split(factor, level)
    far_factor, far_level, _ = lax.optimization_barrier((far_factor, level, own[0]))
    far = split(far_factor, far_level)
    factors = (*own, *far, unlevel[None, :])
    for d in range(3):
        norms = norms + permute(norms, COL_DIMS[d])

    cells = jnp.stack(
        [
            lax.rsqrt(norms),
            scale,
            volatility,
            0.25 * retention.astype(jnp.float32),
            0.25 * limit.astype(jnp.float32),
            cell_entity.astype(jnp.float32),
        ]
    )
    sums = ()
    for c in range(CHUNKS):
        sent, parts = mm(0, tbl, (*gathered[c], *last[c]), factors)
        came = lax.optimization_barrier([permute(sent[q], COL_DIMS[q]) for q in range(3)])
        kept, _ = mm(1, tbl, parts, factors)
        passed = [kept[q][:2] + came[q][:2] for q in range(3)]
        second = lax.optimization_barrier(
            [permute(passed[q], COL_DIMS[(q + 1) % 3]) for q in range(3)]
        )
        passed = [kept[q][2:3] + came[q][2:3] + second[q][:1] for q in range(3)]
        third = lax.optimization_barrier(
            [permute(passed[q], COL_DIMS[(q + 2) % 3]) for q in range(3)]
        )
        held = [kept[q][3:] + came[q][3:] + second[q][1:] for q in range(3)]
        sums = (tail(held, third, cells, sums),)
    parts = lax.all_to_all(sums[0], "row", split_axis=0, concat_axis=0, tiled=True)
    total = jnp.sum(parts, axis=0).reshape(CHUNKS, 2, ROWS, 128)
    return jnp.swapaxes(total, 0, 1).reshape(2, 128, 128)


def solution(mesh):
    return jax.shard_map(
        step,
        mesh=mesh,
        in_specs=(
            P("row", "col"),
            P("row", "col"),
            P("row"),
            P("row"),
            P("row"),
            P("row"),
            P("row"),
        ),
        out_specs=P(None, "col", "row"),
        check_vma=False,
    )
```

```python
import functools

import jax
import jax.numpy as jnp
import numpy as np
from jax import lax
from jax.experimental import pallas as pl
from jax.experimental.pallas import tpu as pltpu
from jax.sharding import PartitionSpec as P


ENT = 1024
CHUNKS = 2
ROWS = 128 // CHUNKS
DEPTH = (768, 640, 640)
DOFF = (0, 768, 1408)
TILE = 256
LIFT = 256.0
COLS = (768, 768, 512)
COFF = (0, 768, 1536)
BOTH = ("row", "col")


def unflat(i):
    row, col = divmod(i, 16)
    return row // 4, row % 4, col // 4, col // 2 % 2, col % 2


def flat(yh, x, z, yl, core):
    return (yh * 4 + x) * 16 + z * 4 + yl * 2 + core


def perm(step):
    return [(i, flat(*step(*unflat(i)))) for i in range(128)]


CORE = perm(lambda yh, x, z, yl, c: (yh, x, z, yl, 1 - c))
ROW_DIMS = (
    perm(lambda yh, x, z, yl, c: (yh, x ^ 1, z, yl, c)),
    perm(lambda yh, x, z, yl, c: (yh, 3 - x, z, yl, c)),
    perm(lambda yh, x, z, yl, c: (1 - yh, x, z, yl, c)),
)
COL_DIMS = (
    perm(lambda yh, x, z, yl, c: (yh, x, z ^ 1, yl, c)),
    perm(lambda yh, x, z, yl, c: (yh, x, 3 - z, yl, c)),
    perm(lambda yh, x, z, yl, c: (yh, x, z, 1 - yl, c)),
)


def gray(v):
    return v ^ (v >> 1)


def ungray(v):
    return (v & 2) | ((v ^ (v >> 1)) & 1)


def place(e, p):
    return sum((e >> (p + s) % 3 & 1) << s for s in range(3))


def tables():
    out = np.zeros((128, 3, 8), np.int32)
    for i in range(128):
        yh, x, z, yl, _ = unflat(i)
        here_r, here_c = gray(x) | yh << 2, gray(z) | yl << 2
        for e in range(8):
            h = here_r ^ e
            source = (h >> 2) * 4 + ungray(h & 3)
            d = (gray(source >> 1) | (source & 1) << 2) ^ here_c
            for q in range(3):
                out[i, q, 7 - sum((d >> (q + s) % 3 & 1) << 2 - s for s in range(3))] = e
    return out.reshape(128, 24)


def permute(x, pairs):
    return lax.ppermute(x, BOTH, pairs)


def split_kernel(x, high, near, rest, norms, unlevel):
    v = x[...]
    h = v.astype(jnp.bfloat16)
    high[...] = h
    total = jnp.sum(v * v, axis=1, keepdims=True)
    fits = total < 3e38
    level = jnp.where(fits, 128.0 * lax.rsqrt(jnp.maximum(total, 1e-30)), 0.0)
    near[...] = (v * level).astype(jnp.float8_e4m3fn)
    rest[...] = ((v - h.astype(jnp.float32)) * (level * LIFT)).astype(jnp.float8_e4m3fn)
    back = jnp.where(fits, 1.0 / (jnp.where(fits, level, 1.0) * LIFT), 0.0)
    norms[...] = jnp.transpose(jnp.broadcast_to(total, (TILE, 128)))[:1]
    unlevel[...] = jnp.transpose(jnp.broadcast_to(back, (TILE, 128)))[:1]


def split(x):
    block = pl.BlockSpec((TILE, 1024), lambda t: (t, 0))
    line = pl.BlockSpec((1, TILE), lambda t: (0, t))
    return pl.pallas_call(
        split_kernel,
        out_shape=[
            jax.ShapeDtypeStruct((2048, 1024), jnp.bfloat16),
            jax.ShapeDtypeStruct((2048, 1024), jnp.float8_e4m3fn),
            jax.ShapeDtypeStruct((2048, 1024), jnp.float8_e4m3fn),
            jax.ShapeDtypeStruct((1, 2048), jnp.float32),
            jax.ShapeDtypeStruct((1, 2048), jnp.float32),
        ],
        grid=(2048 // TILE,),
        in_specs=[block],
        out_specs=[block] * 3 + [line] * 2,
        cost_estimate=pl.CostEstimate(flops=8 * 2**21, bytes_accessed=16 * 2**20, transcendentals=2048),
        compiler_params=pltpu.CompilerParams(vmem_limit_bytes=8 * 2**20),
    )(pltpu.with_memory_space_constraint(x, pltpu.HBM))


STARTS = tuple(c // TILE for c in COFF)
SIZES = tuple(c // TILE for c in COLS)


def mm_kernel(half, tbl, *refs):
    if half == 0:
        first, last, refs = refs[:3], refs[3:6], refs[6:]
    else:
        (high, cross), refs = refs[:2], refs[2:]
    (own16, own8, own_rest, own_level, far16, far8, far_rest, far_level), refs = refs[:8], refs[8:]
    outs, refs = refs[:3], refs[3:]
    t = pl.program_id(0)
    if half == 0:
        high, cross, lhs16, lhs8 = refs

        @pl.when(t == 0)
        def _():
            for e in range(8):
                for p in range(3):
                    at = place(e, p)
                    v = (last if at > 3 else first)[p][at & 3]
                    h = v.astype(jnp.bfloat16)
                    cols = pl.ds(DOFF[p], DEPTH[p])
                    high[e, :, cols] = h
                    cross[0, e, :, cols] = v.astype(jnp.float8_e4m3fn)
                    rest = (v - h.astype(jnp.float32)) * LIFT
                    cross[1, e, :, cols] = rest.astype(jnp.float8_e4m3fn)

    else:
        lhs16, lhs8 = refs
    for q in range(3):

        @pl.when(t == STARTS[q])
        def _(q=q):
            for i in range(4):
                e = tbl[q * 8 + half * 4 + i]
                at = pl.ds(i * ROWS, ROWS)
                lhs16[at, :] = high[e]
                for k in range(2):
                    lhs8[k, at, :] = cross[k, e]

    dot = functools.partial(
        lax.dot_general,
        dimension_numbers=(((1,), (1,)), ((), ())),
        preferred_element_type=jnp.float32,
    )
    own, far = pl.ds(0, 1024), pl.ds(1024, 1024)
    rows = pl.ds(pl.multiple_of(t * TILE, TILE), TILE)
    acc = dot(lhs16[:, own], own16[rows, :]) + dot(lhs16[:, far], far16[rows, :])
    low = dot(lhs8[0, :, own], own_rest[rows, :]) + dot(lhs8[1, :, own], own8[rows, :])
    acc += low * own_level[...]
    low = dot(lhs8[0, :, far], far_rest[rows, :]) + dot(lhs8[1, :, far], far8[rows, :])
    acc = (acc + low * far_level[...]).reshape(4, ROWS, TILE)
    for q in range(3):

        @pl.when((t >= STARTS[q]) & (t < STARTS[q] + SIZES[q]))
        def _(q=q):
            outs[q][...] = acc


def mm(half, tbl, pieces, factors):
    whole = pl.BlockSpec(memory_space=pltpu.VMEM)
    outs = [
        pl.BlockSpec(
            (4, ROWS, TILE), lambda t, tb, q=q: (0, 0, jnp.clip(t - STARTS[q], 0, SIZES[q] - 1))
        )
        for q in range(3)
    ]
    shapes = [jax.ShapeDtypeStruct((4, ROWS, COLS[q]), jnp.float32) for q in range(3)]
    if half == 0:
        outs += [whole] * 2
        shapes += [
            jax.ShapeDtypeStruct((8, ROWS, 2048), jnp.bfloat16),
            jax.ShapeDtypeStruct((2, 8, ROWS, 2048), jnp.float8_e4m3fn),
        ]
    res = pl.pallas_call(
        functools.partial(mm_kernel, half),
        out_shape=shapes,
        grid_spec=pltpu.PrefetchScalarGridSpec(
            num_scalar_prefetch=1,
            grid=(2048 // TILE,),
            in_specs=[whole] * len(pieces) + ([whole] * 3 + [pl.BlockSpec((1, TILE), lambda t, tb: (0, t))]) * 2,
            out_specs=outs,
            scratch_shapes=[
                pltpu.VMEM((4 * ROWS, 2048), jnp.bfloat16),
                pltpu.VMEM((2, 4 * ROWS, 2048), jnp.float8_e4m3fn),
            ],
        ),
        cost_estimate=pl.CostEstimate(
            flops=2 * 2 * 4 * ROWS * 2048 * 2048,
            bytes_accessed=2 * 4 * ROWS * 2048 * 4 + 4 * 2048 * 2048,
            transcendentals=0,
        ),
        compiler_params=pltpu.CompilerParams(vmem_limit_bytes=8 * 2**20),
    )(tbl, *pieces, *factors)
    return res[:3], res[3:]


def tail_kernel(*refs):
    pieces, cells, out, both = refs[:6], refs[6], refs[-2], refs[-1]
    for q in range(3):
        cols = pl.ds(COFF[q], COLS[q])
        mixed = pieces[q][0] + pieces[3 + q][0]
        inv, scale, vol, floor, cover = (cells[pl.ds(k, 1), cols] for k in range(5))
        ground = scale * jnp.exp(vol * (mixed * inv))
        ceded = jnp.minimum(jnp.maximum(ground - floor, 0.0), cover)
        for k, v in enumerate((ground - ceded, ceded)):
            h = v.astype(jnp.bfloat16)
            both[pl.ds(k * ROWS, ROWS), cols] = h
            both[pl.ds((2 + k) * ROWS, ROWS), cols] = (v - h.astype(jnp.float32)).astype(jnp.bfloat16)
    entity = cells[pl.ds(5, 1), :].astype(jnp.int32)
    before = len(refs) == 10
    for g in range(8):
        lines = lax.broadcasted_iota(jnp.int32, (128, 2048), 0) + g * 128
        onehot = jnp.where(lines == entity, 1.0, 0.0).astype(jnp.bfloat16)
        sums = lax.dot_general(
            both[...], onehot, (((1,), (1,)), ((), ())), preferred_element_type=jnp.float32
        )
        sums = sums[: 2 * ROWS] + sums[2 * ROWS :]
        if before:
            out[g, pl.ds(0, 2 * ROWS), :] = refs[7][g]
            out[g, pl.ds(2 * ROWS, 2 * ROWS), :] = sums
        else:
            out[g] = sums


def tail(held, third, cells, before):
    def at(shape):
        return pl.BlockSpec(shape, lambda i: (0,) * len(shape))

    rows = 2 * ROWS * (1 + len(before))
    return pl.pallas_call(
        tail_kernel,
        out_shape=jax.ShapeDtypeStruct((8, rows, 128), jnp.float32),
        grid=(1,),
        in_specs=[at((1, ROWS, COLS[q])) for q in range(3)] * 2
        + [at((6, 2048))]
        + [at((8, 2 * ROWS, 128))] * len(before),
        out_specs=at((8, rows, 128)),
        scratch_shapes=[pltpu.VMEM((4 * ROWS, 2048), jnp.bfloat16)],
        cost_estimate=pl.CostEstimate(
            flops=2 * 4 * ROWS * 2048 * ENT, bytes_accessed=5 * ROWS * 2048 * 4, transcendentals=ROWS * 2048
        ),
        compiler_params=pltpu.CompilerParams(vmem_limit_bytes=16 * 2**20),
    )(*held, *third, cells, *before)


def step(normals, factor, cell_entity, scale, volatility, retention, limit):
    row, col = lax.axis_index("row"), lax.axis_index("col")
    core = col & 1
    tbl = lax.dynamic_index_in_dim(jnp.asarray(tables()), row * 16 + col, 0, False)

    given = permute(lax.dynamic_slice_in_dim(normals, (1 - core) * 128, 128, 0), CORE)
    kept = lax.dynamic_slice_in_dim(normals, core * 128, 128, 0)
    factor, given = lax.optimization_barrier((factor, given))
    far_factor = permute(factor, CORE)
    block = jnp.concatenate([kept[:, DEPTH[0] :], given], axis=1)
    first = [kept[None, c * ROWS : (c + 1) * ROWS, : DEPTH[0]] for c in range(CHUNKS)]
    gathered = [
        [
            first[c],
            block[None, c * ROWS : (c + 1) * ROWS, : DEPTH[1]],
            block[None, c * ROWS : (c + 1) * ROWS, DEPTH[1] :],
        ]
        for c in range(CHUNKS)
    ]
    last = []
    for s in range(3):
        for c in range(CHUNKS):
            came = lax.optimization_barrier([permute(gathered[c][p], ROW_DIMS[(p + s) % 3]) for p in range(3)])
            if s == 2:
                last.append(came)
                continue
            gathered[c] = [jnp.concatenate([gathered[c][p], came[p]], axis=0) for p in range(3)]

    *own, own_norms, own_level = split(factor)
    *far, far_norms, far_level = split(far_factor)
    factors = (*own, own_level, *far, far_level)
    norms = (own_norms + far_norms).reshape(2048)
    for d in range(3):
        norms = norms + permute(norms, COL_DIMS[d])

    cells = jnp.stack(
        [
            lax.rsqrt(norms),
            scale,
            volatility,
            0.25 * retention.astype(jnp.float32),
            0.25 * limit.astype(jnp.float32),
            cell_entity.astype(jnp.float32),
        ]
    )
    sums = ()
    for c in range(CHUNKS):
        sent, parts = mm(0, tbl, (*gathered[c], *last[c]), factors)
        came = lax.optimization_barrier([permute(sent[q], COL_DIMS[q]) for q in range(3)])
        kept, _ = mm(1, tbl, parts, factors)
        passed = [kept[q][:2] + came[q][:2] for q in range(3)]
        second = lax.optimization_barrier([permute(passed[q], COL_DIMS[(q + 1) % 3]) for q in range(3)])
        passed = [kept[q][2:3] + came[q][2:3] + second[q][:1] for q in range(3)]
        third = lax.optimization_barrier([permute(passed[q], COL_DIMS[(q + 2) % 3]) for q in range(3)])
        held = [kept[q][3:] + came[q][3:] + second[q][1:] for q in range(3)]
        sums = (tail(held, third, cells, sums),)
    parts = lax.all_to_all(sums[0], "row", split_axis=0, concat_axis=0, tiled=True)
    total = jnp.sum(parts, axis=0).reshape(CHUNKS, 2, ROWS, 128)
    return jnp.swapaxes(total, 0, 1).reshape(2, 128, 128)


def solution(mesh):
    return jax.shard_map(
        step,
        mesh=mesh,
        in_specs=(
            P("row", "col"),
            P("row", "col"),
            P("row"),
            P("row"),
            P("row"),
            P("row"),
            P("row"),
        ),
        out_specs=P(None, "col", "row"),
        check_vma=False,
    )
```

```python
import functools

import jax
import jax.numpy as jnp
import numpy as np
from jax import lax
from jax.experimental import pallas as pl
from jax.experimental.pallas import tpu as pltpu
from jax.sharding import PartitionSpec as P


ENT = 1024
CHUNKS = 2
ROWS = 128 // CHUNKS
DEPTH = (768, 640, 640)
DOFF = (0, 768, 1408)
TILE = 256
LIFT = 256.0
COLS = (768, 768, 512)
COFF = (0, 768, 1536)
BOTH = ("row", "col")


def unflat(i):
    row, col = divmod(i, 16)
    return row // 4, row % 4, col // 4, col // 2 % 2, col % 2


def flat(yh, x, z, yl, core):
    return (yh * 4 + x) * 16 + z * 4 + yl * 2 + core


def perm(step):
    return [(i, flat(*step(*unflat(i)))) for i in range(128)]


CORE = perm(lambda yh, x, z, yl, c: (yh, x, z, yl, 1 - c))
ROW_DIMS = (
    perm(lambda yh, x, z, yl, c: (yh, x ^ 1, z, yl, c)),
    perm(lambda yh, x, z, yl, c: (yh, 3 - x, z, yl, c)),
    perm(lambda yh, x, z, yl, c: (1 - yh, x, z, yl, c)),
)
COL_DIMS = (
    perm(lambda yh, x, z, yl, c: (yh, x, z ^ 1, yl, c)),
    perm(lambda yh, x, z, yl, c: (yh, x, 3 - z, yl, c)),
    perm(lambda yh, x, z, yl, c: (yh, x, z, 1 - yl, c)),
)


def gray(v):
    return v ^ (v >> 1)


def ungray(v):
    return (v & 2) | ((v ^ (v >> 1)) & 1)


def place(e, p):
    return sum((e >> (p + s) % 3 & 1) << s for s in range(3))


def tables():
    out = np.zeros((128, 3, 8), np.int32)
    for i in range(128):
        yh, x, z, yl, _ = unflat(i)
        here_r, here_c = gray(x) | yh << 2, gray(z) | yl << 2
        for e in range(8):
            h = here_r ^ e
            source = (h >> 2) * 4 + ungray(h & 3)
            d = (gray(source >> 1) | (source & 1) << 2) ^ here_c
            for q in range(3):
                out[i, q, 7 - sum((d >> (q + s) % 3 & 1) << 2 - s for s in range(3))] = e
    return out.reshape(128, 24)


def permute(x, pairs):
    return lax.ppermute(x, BOTH, pairs)


def split(x, level):
    high = lax.reduce_precision(x, 8, 7)
    return (
        high.astype(jnp.bfloat16),
        (high * level[:, None]).astype(jnp.float8_e4m3fn),
        ((x - high) * (level * LIFT)[:, None]).astype(jnp.float8_e4m3fn),
    )


STARTS = tuple(c // TILE for c in COFF)
SIZES = tuple(c // TILE for c in COLS)


def mm_kernel(half, tbl, *refs):
    if half == 0:
        first, last, refs = refs[:3], refs[3:6], refs[6:]
    else:
        (high, cross), refs = refs[:2], refs[2:]
    (own16, own8, own_rest, far16, far8, far_rest, level), refs = refs[:7], refs[7:]
    outs, refs = refs[:3], refs[3:]
    t = pl.program_id(0)
    if half == 0:
        high, cross, lhs16, lhs8 = refs

        @pl.when(t == 0)
        def _():
            for e in range(8):
                for p in range(3):
                    at = place(e, p)
                    v = (last if at > 3 else first)[p][at & 3]
                    h = v.astype(jnp.bfloat16)
                    cols = pl.ds(DOFF[p], DEPTH[p])
                    high[e, :, cols] = h
                    cross[0, e, :, cols] = v.astype(jnp.float8_e4m3fn)
                    rest = (v - h.astype(jnp.float32)) * LIFT
                    cross[1, e, :, cols] = rest.astype(jnp.float8_e4m3fn)

    else:
        lhs16, lhs8 = refs
    for q in range(3):

        @pl.when(t == STARTS[q])
        def _(q=q):
            for i in range(4):
                e = tbl[q * 8 + half * 4 + i]
                at = pl.ds(i * ROWS, ROWS)
                lhs16[at, :] = high[e]
                for k in range(2):
                    lhs8[k, at, :] = cross[k, e]

    dot = functools.partial(
        lax.dot_general,
        dimension_numbers=(((1,), (1,)), ((), ())),
        preferred_element_type=jnp.float32,
    )
    own, far = pl.ds(0, 1024), pl.ds(1024, 1024)
    rows = pl.ds(pl.multiple_of(t * TILE, TILE), TILE)
    acc = dot(lhs16[:, own], own16[rows, :]) + dot(lhs16[:, far], far16[rows, :])
    low = dot(lhs8[0, :, own], own_rest[rows, :]) + dot(lhs8[0, :, far], far_rest[rows, :])
    low += dot(lhs8[1, :, own], own8[rows, :]) + dot(lhs8[1, :, far], far8[rows, :])
    acc = (acc + low * level[...]).reshape(4, ROWS, TILE)
    for q in range(3):

        @pl.when((t >= STARTS[q]) & (t < STARTS[q] + SIZES[q]))
        def _(q=q):
            outs[q][...] = acc


def mm(half, tbl, pieces, factors):
    whole = pl.BlockSpec(memory_space=pltpu.VMEM)
    outs = [
        pl.BlockSpec(
            (4, ROWS, TILE), lambda t, tb, q=q: (0, 0, jnp.clip(t - STARTS[q], 0, SIZES[q] - 1))
        )
        for q in range(3)
    ]
    shapes = [jax.ShapeDtypeStruct((4, ROWS, COLS[q]), jnp.float32) for q in range(3)]
    if half == 0:
        outs += [whole] * 2
        shapes += [
            jax.ShapeDtypeStruct((8, ROWS, 2048), jnp.bfloat16),
            jax.ShapeDtypeStruct((2, 8, ROWS, 2048), jnp.float8_e4m3fn),
        ]
    res = pl.pallas_call(
        functools.partial(mm_kernel, half),
        out_shape=shapes,
        grid_spec=pltpu.PrefetchScalarGridSpec(
            num_scalar_prefetch=1,
            grid=(2048 // TILE,),
            in_specs=[whole] * (len(pieces) + 6) + [pl.BlockSpec((1, TILE), lambda t, tb: (0, t))],
            out_specs=outs,
            scratch_shapes=[
                pltpu.VMEM((4 * ROWS, 2048), jnp.bfloat16),
                pltpu.VMEM((2, 4 * ROWS, 2048), jnp.float8_e4m3fn),
            ],
        ),
        cost_estimate=pl.CostEstimate(
            flops=2 * 2 * 4 * ROWS * 2048 * 2048,
            bytes_accessed=2 * 4 * ROWS * 2048 * 4 + 4 * 2048 * 2048,
            transcendentals=0,
        ),
        compiler_params=pltpu.CompilerParams(vmem_limit_bytes=8 * 2**20),
    )(tbl, *pieces, *factors)
    return res[:3], res[3:]


def tail_kernel(*refs):
    pieces, cells, out, both = refs[:6], refs[6], refs[-2], refs[-1]
    for q in range(3):
        cols = pl.ds(COFF[q], COLS[q])
        mixed = pieces[q][0] + pieces[3 + q][0]
        inv, scale, vol, floor, cover = (cells[pl.ds(k, 1), cols] for k in range(5))
        ground = scale * jnp.exp(vol * (mixed * inv))
        ceded = jnp.minimum(jnp.maximum(ground - floor, 0.0), cover)
        for k, v in enumerate((ground - ceded, ceded)):
            h = v.astype(jnp.bfloat16)
            both[pl.ds(k * ROWS, ROWS), cols] = h
            both[pl.ds((2 + k) * ROWS, ROWS), cols] = (v - h.astype(jnp.float32)).astype(jnp.bfloat16)
    entity = cells[pl.ds(5, 1), :].astype(jnp.int32)
    before = len(refs) == 10
    for g in range(8):
        lines = lax.broadcasted_iota(jnp.int32, (128, 2048), 0) + g * 128
        onehot = jnp.where(lines == entity, 1.0, 0.0).astype(jnp.bfloat16)
        sums = lax.dot_general(
            both[...], onehot, (((1,), (1,)), ((), ())), preferred_element_type=jnp.float32
        )
        sums = sums[: 2 * ROWS] + sums[2 * ROWS :]
        if before:
            out[g, pl.ds(0, 2 * ROWS), :] = refs[7][g]
            out[g, pl.ds(2 * ROWS, 2 * ROWS), :] = sums
        else:
            out[g] = sums


def tail(held, third, cells, before):
    def at(shape):
        return pl.BlockSpec(shape, lambda i: (0,) * len(shape))

    rows = 2 * ROWS * (1 + len(before))
    return pl.pallas_call(
        tail_kernel,
        out_shape=jax.ShapeDtypeStruct((8, rows, 128), jnp.float32),
        grid=(1,),
        in_specs=[at((1, ROWS, COLS[q])) for q in range(3)] * 2
        + [at((6, 2048))]
        + [at((8, 2 * ROWS, 128))] * len(before),
        out_specs=at((8, rows, 128)),
        scratch_shapes=[pltpu.VMEM((4 * ROWS, 2048), jnp.bfloat16)],
        cost_estimate=pl.CostEstimate(
            flops=2 * 4 * ROWS * 2048 * ENT, bytes_accessed=5 * ROWS * 2048 * 4, transcendentals=ROWS * 2048
        ),
        compiler_params=pltpu.CompilerParams(vmem_limit_bytes=16 * 2**20),
    )(*held, *third, cells, *before)


def step(normals, factor, cell_entity, scale, volatility, retention, limit):
    row, col = lax.axis_index("row"), lax.axis_index("col")
    core = col & 1
    tbl = lax.dynamic_index_in_dim(jnp.asarray(tables()), row * 16 + col, 0, False)

    given = permute(lax.dynamic_slice_in_dim(normals, (1 - core) * 128, 128, 0), CORE)
    kept = lax.dynamic_slice_in_dim(normals, core * 128, 128, 0)
    factor, given = lax.optimization_barrier((factor, given))
    far_factor = permute(factor, CORE)
    block = jnp.concatenate([kept[:, DEPTH[0] :], given], axis=1)
    first = [kept[None, c * ROWS : (c + 1) * ROWS, : DEPTH[0]] for c in range(CHUNKS)]
    gathered = [
        [
            first[c],
            block[None, c * ROWS : (c + 1) * ROWS, : DEPTH[1]],
            block[None, c * ROWS : (c + 1) * ROWS, DEPTH[1] :],
        ]
        for c in range(CHUNKS)
    ]
    last = []
    for s in range(3):
        for c in range(CHUNKS):
            came = lax.optimization_barrier(
                [permute(gathered[c][p], ROW_DIMS[(p + s) % 3]) for p in range(3)]
            )
            if s == 2:
                last.append(came)
                continue
            gathered[c] = [jnp.concatenate([gathered[c][p], came[p]], axis=0) for p in range(3)]

    norms = jnp.sum(factor * factor, axis=1)
    norms = norms + permute(norms, CORE)
    fits = norms < 3e38
    level = 128.0 * lax.rsqrt(jnp.where(fits, jnp.maximum(norms, 1e-30), 1.0))
    unlevel = jnp.where(fits, 1.0 / (level * LIFT), 0.0)
    level, unlevel, norms = lax.optimization_barrier((jnp.where(fits, level, 0.0), unlevel, norms))
    own = split(factor, level)
    far_factor, far_level, _ = lax.optimization_barrier((far_factor, level, own[0]))
    far = split(far_factor, far_level)
    factors = (*own, *far, unlevel[None, :])
    for d in range(3):
        norms = norms + permute(norms, COL_DIMS[d])

    cells = jnp.stack(
        [
            lax.rsqrt(norms),
            scale,
            volatility,
            0.25 * retention.astype(jnp.float32),
            0.25 * limit.astype(jnp.float32),
            cell_entity.astype(jnp.float32),
        ]
    )
    sums = ()
    for c in range(CHUNKS):
        sent, parts = mm(0, tbl, (*gathered[c], *last[c]), factors)
        came = lax.optimization_barrier([permute(sent[q], COL_DIMS[q]) for q in range(3)])
        kept, _ = mm(1, tbl, parts, factors)
        passed = [kept[q][:2] + came[q][:2] for q in range(3)]
        second = lax.optimization_barrier(
            [permute(passed[q], COL_DIMS[(q + 1) % 3]) for q in range(3)]
        )
        passed = [kept[q][2:3] + came[q][2:3] + second[q][:1] for q in range(3)]
        third = lax.optimization_barrier(
            [permute(passed[q], COL_DIMS[(q + 2) % 3]) for q in range(3)]
        )
        held = [kept[q][3:] + came[q][3:] + second[q][1:] for q in range(3)]
        sums = (tail(held, third, cells, sums),)
    parts = lax.all_to_all(sums[0], "row", split_axis=0, concat_axis=0, tiled=True)
    total = jnp.sum(parts, axis=0).reshape(CHUNKS, 2, ROWS, 128)
    return jnp.swapaxes(total, 0, 1).reshape(2, 128, 128)


def solution(mesh):
    return jax.shard_map(
        step,
        mesh=mesh,
        in_specs=(
            P("row", "col"),
            P("row", "col"),
            P("row"),
            P("row"),
            P("row"),
            P("row"),
            P("row"),
        ),
        out_specs=P(None, "col", "row"),
        check_vma=False,
    )
```

```python
import functools

import jax
import jax.numpy as jnp
import numpy as np
from jax import lax
from jax.experimental import pallas as pl
from jax.experimental.pallas import tpu as pltpu
from jax.sharding import PartitionSpec as P


ENT = 1024
CHUNKS = 2
ROWS = 128 // CHUNKS
DEPTH = (768, 640, 640)
DOFF = (0, 768, 1408)
TILE = 256
LIFT = 256.0
COLS = (768, 768, 512)
COFF = (0, 768, 1536)
BOTH = ("row", "col")


def unflat(i):
    row, col = divmod(i, 16)
    return row // 4, row % 4, col // 4, col // 2 % 2, col % 2


def flat(yh, x, z, yl, core):
    return (yh * 4 + x) * 16 + z * 4 + yl * 2 + core


def perm(step):
    return [(i, flat(*step(*unflat(i)))) for i in range(128)]


CORE = perm(lambda yh, x, z, yl, c: (yh, x, z, yl, 1 - c))
ROW_DIMS = (
    perm(lambda yh, x, z, yl, c: (yh, x ^ 1, z, yl, c)),
    perm(lambda yh, x, z, yl, c: (yh, 3 - x, z, yl, c)),
    perm(lambda yh, x, z, yl, c: (1 - yh, x, z, yl, c)),
)
COL_DIMS = (
    perm(lambda yh, x, z, yl, c: (yh, x, z ^ 1, yl, c)),
    perm(lambda yh, x, z, yl, c: (yh, x, 3 - z, yl, c)),
    perm(lambda yh, x, z, yl, c: (yh, x, z, 1 - yl, c)),
)


def gray(v):
    return v ^ (v >> 1)


def ungray(v):
    return (v & 2) | ((v ^ (v >> 1)) & 1)


def place(e, p):
    return sum((e >> (p + s) % 3 & 1) << s for s in range(3))


def tables():
    out = np.zeros((128, 3, 8), np.int32)
    for i in range(128):
        yh, x, z, yl, _ = unflat(i)
        here_r, here_c = gray(x) | yh << 2, gray(z) | yl << 2
        for e in range(8):
            h = here_r ^ e
            source = (h >> 2) * 4 + ungray(h & 3)
            d = (gray(source >> 1) | (source & 1) << 2) ^ here_c
            for q in range(3):
                out[i, q, 7 - sum((d >> (q + s) % 3 & 1) << 2 - s for s in range(3))] = e
    return out.reshape(128, 24)


def permute(x, pairs):
    return lax.ppermute(x, BOTH, pairs)


def split(x, level):
    high = lax.reduce_precision(x, 8, 7)
    return (
        high.astype(jnp.bfloat16),
        (high * level[:, None]).astype(jnp.float8_e4m3fn),
        ((x - high) * (level * LIFT)[:, None]).astype(jnp.float8_e4m3fn),
    )


STARTS = tuple(c // TILE for c in COFF)
SIZES = tuple(c // TILE for c in COLS)


def mm_kernel(half, qs, tbl, *refs):
    fresh = half == 0 and qs[0] == 0
    if fresh:
        first, last, refs = refs[:3], refs[3:6], refs[6:]
    else:
        (high, cross), refs = refs[:2], refs[2:]
    (own16, own8, own_rest, far16, far8, far_rest, level), refs = refs[:7], refs[7:]
    outs, refs = refs[: len(qs)], refs[len(qs) :]
    t = pl.program_id(0) + STARTS[qs[0]]
    if fresh:
        high, cross, lhs16, lhs8 = refs

        @pl.when(t == 0)
        def _():
            for e in range(8):
                for p in range(3):
                    at = place(e, p)
                    v = (last if at > 3 else first)[p][at & 3]
                    h = v.astype(jnp.bfloat16)
                    cols = pl.ds(DOFF[p], DEPTH[p])
                    high[e, :, cols] = h
                    cross[0, e, :, cols] = v.astype(jnp.float8_e4m3fn)
                    rest = (v - h.astype(jnp.float32)) * LIFT
                    cross[1, e, :, cols] = rest.astype(jnp.float8_e4m3fn)

    else:
        lhs16, lhs8 = refs
    for q in qs:

        @pl.when(t == STARTS[q])
        def _(q=q):
            for i in range(4):
                e = tbl[q * 8 + half * 4 + i]
                at = pl.ds(i * ROWS, ROWS)
                lhs16[at, :] = high[e]
                for k in range(2):
                    lhs8[k, at, :] = cross[k, e]

    dot = functools.partial(
        lax.dot_general,
        dimension_numbers=(((1,), (1,)), ((), ())),
        preferred_element_type=jnp.float32,
    )
    own, far = pl.ds(0, 1024), pl.ds(1024, 1024)
    rows = pl.ds(pl.multiple_of(t * TILE, TILE), TILE)
    acc = dot(lhs16[:, own], own16[rows, :]) + dot(lhs16[:, far], far16[rows, :])
    low = dot(lhs8[0, :, own], own_rest[rows, :]) + dot(lhs8[0, :, far], far_rest[rows, :])
    low += dot(lhs8[1, :, own], own8[rows, :]) + dot(lhs8[1, :, far], far8[rows, :])
    acc = (acc + low * level[...]).reshape(4, ROWS, TILE)
    for k, q in enumerate(qs):

        @pl.when((t >= STARTS[q]) & (t < STARTS[q] + SIZES[q]))
        def _(k=k):
            outs[k][...] = acc


def mm(half, qs, tbl, pieces, factors):
    start = STARTS[qs[0]]
    whole = pl.BlockSpec(memory_space=pltpu.VMEM)
    outs = [
        pl.BlockSpec(
            (4, ROWS, TILE), lambda t, tb, q=q: (0, 0, jnp.clip(t + start - STARTS[q], 0, SIZES[q] - 1))
        )
        for q in qs
    ]
    shapes = [jax.ShapeDtypeStruct((4, ROWS, COLS[q]), jnp.float32) for q in qs]
    tiles = sum(SIZES[q] for q in qs)
    if half == 0 and qs[0] == 0:
        outs += [whole] * 2
        shapes += [
            jax.ShapeDtypeStruct((8, ROWS, 2048), jnp.bfloat16),
            jax.ShapeDtypeStruct((2, 8, ROWS, 2048), jnp.float8_e4m3fn),
        ]
    res = pl.pallas_call(
        functools.partial(mm_kernel, half, qs),
        out_shape=shapes,
        grid_spec=pltpu.PrefetchScalarGridSpec(
            num_scalar_prefetch=1,
            grid=(tiles,),
            in_specs=[whole] * (len(pieces) + 6) + [pl.BlockSpec((1, TILE), lambda t, tb: (0, t + start))],
            out_specs=outs,
            scratch_shapes=[
                pltpu.VMEM((4 * ROWS, 2048), jnp.bfloat16),
                pltpu.VMEM((2, 4 * ROWS, 2048), jnp.float8_e4m3fn),
            ],
        ),
        cost_estimate=pl.CostEstimate(
            flops=2 * 2 * 4 * ROWS * 2048 * tiles * TILE,
            bytes_accessed=4 * ROWS * 2048 * 4 + tiles * TILE * (4 * 2048 + 16 * ROWS),
            transcendentals=0,
        ),
        compiler_params=pltpu.CompilerParams(vmem_limit_bytes=8 * 2**20),
    )(tbl, *pieces, *factors)
    return res[: len(qs)], res[len(qs) :]


def tail_kernel(*refs):
    pieces, cells, out, both = refs[:6], refs[6], refs[-2], refs[-1]
    for q in range(3):
        cols = pl.ds(COFF[q], COLS[q])
        mixed = pieces[q][0] + pieces[3 + q][0]
        inv, scale, vol, floor, cover = (cells[pl.ds(k, 1), cols] for k in range(5))
        ground = scale * jnp.exp(vol * (mixed * inv))
        ceded = jnp.minimum(jnp.maximum(ground - floor, 0.0), cover)
        for k, v in enumerate((ground - ceded, ceded)):
            h = v.astype(jnp.bfloat16)
            both[pl.ds(k * ROWS, ROWS), cols] = h
            both[pl.ds((2 + k) * ROWS, ROWS), cols] = (v - h.astype(jnp.float32)).astype(jnp.bfloat16)
    entity = cells[pl.ds(5, 1), :].astype(jnp.int32)
    before = len(refs) == 10
    for g in range(8):
        lines = lax.broadcasted_iota(jnp.int32, (128, 2048), 0) + g * 128
        onehot = jnp.where(lines == entity, 1.0, 0.0).astype(jnp.bfloat16)
        sums = lax.dot_general(
            both[...], onehot, (((1,), (1,)), ((), ())), preferred_element_type=jnp.float32
        )
        sums = sums[: 2 * ROWS] + sums[2 * ROWS :]
        if before:
            out[g, pl.ds(0, 2 * ROWS), :] = refs[7][g]
            out[g, pl.ds(2 * ROWS, 2 * ROWS), :] = sums
        else:
            out[g] = sums


def tail(held, third, cells, before):
    def at(shape):
        return pl.BlockSpec(shape, lambda i: (0,) * len(shape))

    rows = 2 * ROWS * (1 + len(before))
    return pl.pallas_call(
        tail_kernel,
        out_shape=jax.ShapeDtypeStruct((8, rows, 128), jnp.float32),
        grid=(1,),
        in_specs=[at((1, ROWS, COLS[q])) for q in range(3)] * 2
        + [at((6, 2048))]
        + [at((8, 2 * ROWS, 128))] * len(before),
        out_specs=at((8, rows, 128)),
        scratch_shapes=[pltpu.VMEM((4 * ROWS, 2048), jnp.bfloat16)],
        cost_estimate=pl.CostEstimate(
            flops=2 * 4 * ROWS * 2048 * ENT, bytes_accessed=5 * ROWS * 2048 * 4, transcendentals=ROWS * 2048
        ),
        compiler_params=pltpu.CompilerParams(vmem_limit_bytes=16 * 2**20),
    )(*held, *third, cells, *before)


def step(normals, factor, cell_entity, scale, volatility, retention, limit):
    row, col = lax.axis_index("row"), lax.axis_index("col")
    core = col & 1
    tbl = lax.dynamic_index_in_dim(jnp.asarray(tables()), row * 16 + col, 0, False)

    given = permute(lax.dynamic_slice_in_dim(normals, (1 - core) * 128, 128, 0), CORE)
    kept = lax.dynamic_slice_in_dim(normals, core * 128, 128, 0)
    factor, given = lax.optimization_barrier((factor, given))
    far_factor = permute(factor, CORE)
    block = jnp.concatenate([kept[:, DEPTH[0] :], given], axis=1)
    first = [kept[None, c * ROWS : (c + 1) * ROWS, : DEPTH[0]] for c in range(CHUNKS)]
    gathered = [
        [
            first[c],
            block[None, c * ROWS : (c + 1) * ROWS, : DEPTH[1]],
            block[None, c * ROWS : (c + 1) * ROWS, DEPTH[1] :],
        ]
        for c in range(CHUNKS)
    ]
    last = []
    for s in range(3):
        for c in range(CHUNKS):
            came = lax.optimization_barrier([permute(gathered[c][p], ROW_DIMS[(p + s) % 3]) for p in range(3)])
            if s == 2:
                last.append(came)
                continue
            gathered[c] = [jnp.concatenate([gathered[c][p], came[p]], axis=0) for p in range(3)]

    norms = jnp.sum(factor * factor, axis=1)
    norms = norms + permute(norms, CORE)
    fits = norms < 3e38
    level = 128.0 * lax.rsqrt(jnp.where(fits, jnp.maximum(norms, 1e-30), 1.0))
    unlevel = jnp.where(fits, 1.0 / (level * LIFT), 0.0)
    level, unlevel, norms = lax.optimization_barrier((jnp.where(fits, level, 0.0), unlevel, norms))
    own = split(factor, level)
    far_factor, far_level, _ = lax.optimization_barrier((far_factor, level, own[0]))
    far = split(far_factor, far_level)
    factors = (*own, *far, unlevel[None, :])
    for d in range(3):
        norms = norms + permute(norms, COL_DIMS[d])

    cells = jnp.stack(
        [
            lax.rsqrt(norms),
            scale,
            volatility,
            0.25 * retention.astype(jnp.float32),
            0.25 * limit.astype(jnp.float32),
            cell_entity.astype(jnp.float32),
        ]
    )
    sums = ()
    for c in range(CHUNKS):
        sent, parts = mm(0, (0,), tbl, (*gathered[c], *last[c]), factors)
        sent = [*sent, *mm(0, (1, 2), tbl, parts, factors)[0]]
        came = lax.optimization_barrier([permute(sent[q], COL_DIMS[q]) for q in range(3)])
        kept, _ = mm(1, (0, 1, 2), tbl, parts, factors)
        passed = [kept[q][:2] + came[q][:2] for q in range(3)]
        second = lax.optimization_barrier([permute(passed[q], COL_DIMS[(q + 1) % 3]) for q in range(3)])
        passed = [kept[q][2:3] + came[q][2:3] + second[q][:1] for q in range(3)]
        third = lax.optimization_barrier([permute(passed[q], COL_DIMS[(q + 2) % 3]) for q in range(3)])
        held = [kept[q][3:] + came[q][3:] + second[q][1:] for q in range(3)]
        sums = (tail(held, third, cells, sums),)
    parts = lax.all_to_all(sums[0], "row", split_axis=0, concat_axis=0, tiled=True)
    total = jnp.sum(parts, axis=0).reshape(CHUNKS, 2, ROWS, 128)
    return jnp.swapaxes(total, 0, 1).reshape(2, 128, 128)


def solution(mesh):
    return jax.shard_map(
        step,
        mesh=mesh,
        in_specs=(
            P("row", "col"),
            P("row", "col"),
            P("row"),
            P("row"),
            P("row"),
            P("row"),
            P("row"),
        ),
        out_specs=P(None, "col", "row"),
        check_vma=False,
    )
```
